256 devices in a mesh: expert: 32 (over x, z), tensor: 8 (over y, core).
Axes of the slice: x: 4, y: 4, z: 8, core: 2. Of those that a mesh axis runs over, the one named last changes fastest.
Arguments:
- tokens: bfloat16 [8192, 4096], P('expert'), may hold values from -6 to 6
- cotangent: bfloat16 [8192, 4096], P('expert'), may hold values from -1.5 to 1.5
- w_in: bfloat16 [4096, 65536], P(None, ('expert', 'tensor')), may hold values from -0.09375 to 0.09375
- w_out: bfloat16 [65536, 4096], P(('expert', 'tensor')), may hold values from -0.09375 to 0.09375
- router: bfloat16 [4096, 16], replicated, may hold values from -0.09375 to 0.09375
- chosen: int32 [16, 512], replicated, may hold values from 0 to 8191, as said below
Outputs:
- grad_tokens: bfloat16 [8192, 4096], P('expert', 'tensor')
- grad_in: bfloat16 [4096, 65536], P(None, ('expert', 'tensor'))
- grad_out: bfloat16 [65536, 4096], P(('expert', 'tensor'))
- grad_router: float32 [4096, 16], replicated
The draws below stay inside these ranges and needn't reach their ends.
Inputs may be any that keep to these rules, and one draw needn't show every extreme that they name: Row e lists, in increasing order, 512 distinct tokens chosen by expert e; at most 32 of them lie among one device's 256 consecutive tokens, and in every row some device's tokens hold exactly 32 of them.
All inputs are finite; a program needn't handle non-finite values.
Results may differ from the reference program's by a relative error of at most 0.005.
Values may be sent and summed in bfloat16 or wider, within the bound.
A program may use at most 128 MiB of HBM per device.

```python
import jax
import jax.numpy as jnp
from jax import lax

D = 4096
H = 4096
TOK_DEV = 256
EXPERTS = 16
TOKENS = 8192
CAP = 512
MOST = 32


def draw_chosen(key, part):
    home_count = TOKENS // TOK_DEV

    def one_expert(expert_key):
        order_key, forced_key, rank_key = jax.random.split(expert_key, 3)
        forced = jax.random.randint(forced_key, (), 0, home_count)
        order = jax.random.permutation(order_key, home_count * MOST).astype(jnp.int32)
        grid_home = jnp.arange(home_count * MOST, dtype=jnp.int32) // MOST
        order = jnp.where(grid_home == forced, -1 - order, order)
        slot_rank = jnp.argsort(jnp.argsort(order, stable=True), stable=True)
        taken = (slot_rank < CAP).reshape(home_count, MOST)
        counts = jnp.sum(taken.astype(jnp.int32), axis=1)
        ranks = jax.vmap(lambda row_key: jax.random.permutation(row_key, TOK_DEV))(jax.random.split(rank_key, home_count))
        picked = (ranks < counts[:, None]).reshape(-1)
        return jnp.nonzero(picked, size=CAP)[0].astype(jnp.int32)
    return jax.vmap(one_expert)(jax.random.split(key, EXPERTS))


def steps_of(own_key, shape, shards, least, top_value):
    def one(dim, parts):
        steps = jax.random.uniform(jax.random.fold_in(jax.random.fold_in(own_key, 6), dim), (parts,), jnp.float32, least / len(shards), top_value / len(shards))
        return jnp.repeat(jnp.exp(steps), shape[dim] // parts).reshape((-1,) + (1,) * (len(shape) - dim - 1))

    level = one(*shards[0])
    for cut in shards[1:]:
        level = level * one(*cut)
    return level


def scatter_about(stream_key, dims, scale, reach, shards=(), kind=jnp.bfloat16):
    entries = jax.random.normal(stream_key, dims, jnp.float32) * scale
    if len(shards) > 0:
        entries = steps_of(stream_key, dims, shards, -0.22, 0.18) * entries
    return jnp.clip(entries, min=-reach, max=reach).astype(kind)


def setup_inputs(seed: int = 0) -> dict:
    seeds = jax.random.split(jax.random.key(seed), 7)
    return {
        "tokens": scatter_about(seeds[0], (TOKENS, D), 1.0, 6.0, ((0, 32),)),
        "cotangent": scatter_about(seeds[1], (TOKENS, D), 0.25, 1.5, ((0, 32),)),
        "w_in": scatter_about(seeds[2], (D, EXPERTS * H), D ** -0.5, 0.09375, ((1, 256),)),
        "w_out": scatter_about(seeds[3], (EXPERTS * H, D), H ** -0.5, 0.09375, ((0, 256),)),
        "router": scatter_about(seeds[4], (D, EXPERTS), D ** -0.5, 0.09375),
        "chosen": draw_chosen(jax.random.fold_in(seeds[6], 71), 0),
    }


def reference(tokens, cotangent, w_in, w_out, router, chosen):
    def per_expert(total, expert):
        rows = chosen[expert]
        x_rows = tokens[rows]
        y_rows = cotangent[rows]
        w_first = lax.dynamic_slice_in_dim(w_in, expert * H, H, 1)
        w_second = lax.dynamic_slice_in_dim(w_out, expert * H, H, 0)
        r_col = lax.dynamic_slice_in_dim(router, expert, 1, 1)
        gate = jax.nn.sigmoid(jnp.dot(x_rows, r_col, preferred_element_type=jnp.float32)[:, 0])
        pre_act = jnp.dot(x_rows, w_first, preferred_element_type=jnp.float32)
        sig_act = jax.nn.sigmoid(pre_act)
        hidden = pre_act * sig_act
        upstream = jnp.dot(y_rows, w_second.T, preferred_element_type=jnp.float32)
        gated_hidden = (gate[:, None] * hidden).astype(jnp.bfloat16)
        gate_grad = jnp.sum(hidden * upstream, axis=1)
        pre_grad = (gate[:, None] * upstream * sig_act * (1.0 + pre_act * (1.0 - sig_act))).astype(jnp.bfloat16)
        grad_second = jnp.dot(gated_hidden.T, y_rows, preferred_element_type=jnp.float32).astype(jnp.bfloat16)
        grad_first = jnp.dot(x_rows.T, pre_grad, preferred_element_type=jnp.float32).astype(jnp.bfloat16)
        score_grad = gate_grad * gate * (1.0 - gate)
        router_col = jnp.dot(score_grad, x_rows.astype(jnp.float32), precision=lax.Precision.HIGHEST)
        row_grad = jnp.dot(pre_grad, w_first.T, preferred_element_type=jnp.float32)
        row_grad = row_grad + score_grad[:, None] * r_col[:, 0].astype(jnp.float32)[None, :]
        total = total.at[rows].add(row_grad)
        return total, (grad_first, grad_second, router_col)

    start = jnp.zeros((TOKENS, D), jnp.float32)
    total, (grad_first, grad_second, router_cols) = lax.scan(per_expert, start, jnp.arange(EXPERTS, dtype=jnp.int32))
    grad_tokens = total.astype(jnp.bfloat16)
    grad_in = jnp.transpose(grad_first, (1, 0, 2)).reshape(D, EXPERTS * H)
    grad_out = grad_second.reshape(EXPERTS * H, D)
    grad_router = router_cols.T
    return (grad_tokens, grad_in, grad_out, grad_router)
```

```python
import functools

import jax
import jax.numpy as jnp
from jax import lax
from jax.experimental import pallas as pl
from jax.experimental.pallas import tpu as pltpu
from jax.sharding import PartitionSpec as P

MESH = pl.DeviceIdType.MESH
BF = jnp.bfloat16
F32 = jnp.float32
RING = 4


def mm(a, b, dims):
    return lax.dot_general(a, b, (dims, ((), ())), preferred_element_type=F32)


def step_kernel(
    ne, nt, bucket,
    tok, cot, w_in, w_out, rrow, sel_col, sel_row, q_col, q_row,
    gt, gin, gout, gr,
    tv, w1v, w2v, sx, rx, gx, acc, gp, hg, da, dsb, rb, cb, zb, yi, yj, yk, yl, zf, fv, fb, es, er,
    ginv, goutv, rp, rq, rs1, rz, rv, rw, rxs, ry,
    ld, p1s, p1r, ags, agr, cs, cr, zzs, zzr, yis, yir, yjs, yjr, yks, ykr, yls, ylr, zfs, zfr,
    rets, retr, r1s, r1r, rzs, rzr, r2s, r2r, r3s, r3r, outs,
):
    me = lax.axis_index("expert")
    t = lax.axis_index("tensor")
    h = me % 2
    y = t // 2
    c = t % 2
    feat = tv.shape[2]
    share = feat // 2
    cap = hg.shape[0]
    groups = gx.shape[1]
    half = cap // 2
    quarter = cap // 4

    zdev = (me + 1 - 2 * h, t)
    cdev = (me, 2 * y + 1 - c)
    yn = (y + 1) % RING
    yp = (y + 3) % RING
    yo = (y + 2) % RING
    ynd = (me, 2 * yn + c)
    ypd = (me, 2 * yp + c)

    def rcopy(src, dst, ss, rs, dev):
        return pltpu.make_async_remote_copy(
            src_ref=src, dst_ref=dst, send_sem=ss, recv_sem=rs, device_id=dev, device_id_type=MESH
        )

    pending = []

    def send(src, dst, ss, rs, dev):
        copy = rcopy(src, dst, ss, rs, dev)
        copy.start()
        pending.append(copy)

    def arrived(dst, rs):
        rcopy(dst, dst, rs, rs, zdev).wait_recv()

    loads = [
        pltpu.make_async_copy(tok.at[:, pl.ds(pl.multiple_of(t * feat, feat), feat)], tv.at[0], ld.at[0]),
        pltpu.make_async_copy(cot.at[:, pl.ds(pl.multiple_of(t * feat, feat), feat)], tv.at[1], ld.at[1]),
        pltpu.make_async_copy(w_in, w1v, ld.at[2]),
        pltpu.make_async_copy(w_out, w2v, ld.at[3]),
    ]
    for load in loads:
        load.start()

    barrier = pltpu.get_barrier_semaphore()

    @pl.loop(1, ne)
    def _(d):
        pl.semaphore_signal(barrier, inc=1, device_id=((me + d) % ne, t), device_id_type=MESH)

    @pl.loop(1, nt)
    def _(d):
        pl.semaphore_signal(barrier, inc=1, device_id=(me, (t + d) % nt), device_id_type=MESH)

    slots = sel_col.shape[0]
    hot = (lax.broadcasted_iota(jnp.int32, (slots, tv.shape[1]), 1) == sel_col[...]).astype(BF)

    for a in range(2):
        loads[a].wait()
        for k in range(2):
            packed = mm(hot, tv[a, :, k * share:(k + 1) * share], ((1,), (0,))).astype(BF)
            sx[a, :, k] = packed.reshape(slots // bucket, bucket, share)
        if a == 0:
            pl.semaphore_wait(barrier, ne + nt - 2)

        @pl.loop(1, ne)
        def _(d):
            to = (me + d) % ne
            rcopy(sx.at[a, to // 2, to % 2], rx.at[a, me], p1s.at[a, to], p1r.at[a, me], (to, t)).start()

        rx[a, me] = sx[a, me // 2, h]

    def own(a, y_, h_):
        return gx.at[a, 4 * y_ + 2 * c + h_]

    own_g = 4 * y + 2 * c + h

    def fan(a, y_, h_, target, part=None):
        g = 4 * y_ + 2 * c + h_
        j = 2 * y_ + h_
        dev = (zdev, ynd, ypd, cdev)[target]
        if part is None:
            ref = gx.at[a, g]
            send(ref, ref, ags.at[a, j, 0, target], agr.at[a, g, 0], dev)
        else:
            ref = gx.at[a, g, pl.ds(part * half, half)]
            send(ref, ref, ags.at[a, j, part, target], agr.at[a, g, part], dev)

    def got(a, y_, h_):
        g = 4 * y_ + 2 * c + h_
        arrived(gx.at[a, g], agr.at[a, g, 0])

    def got_halves(a, y_, h_):
        g = 4 * y_ + 2 * c + h_
        for part in range(2):
            arrived(gx.at[a, g, pl.ds(part * half, half)], agr.at[a, g, part])

    Z, N, B, C = 0, 1, 2, 3
    rows = 128

    def compact(a):
        @pl.loop(1, ne)
        def _(d):
            source = (me + ne - d) % ne
            arrived(rx.at[a, source], p1r.at[a, source])

        buckets = ne * bucket

        @pl.loop(0, cap // rows)
        def _(i):
            at = pl.ds(pl.multiple_of(i * rows, rows), rows)
            pick = (lax.broadcasted_iota(jnp.int32, (rows, buckets), 1) == q_col[at, :]).astype(BF)
            gx[a, own_g, at] = mm(pick, rx[a].reshape(buckets, share), ((1,), (0,))).astype(BF)

    acc[...] = jnp.zeros_like(acc)
    gp[...] = jnp.zeros_like(gp)

    def block_at(g):
        return pl.ds(pl.multiple_of(g * share, share), share)

    def add_x(g):
        x = gx[0, g]
        acc[0] += mm(x, w1v[block_at(g), :], ((1,), (0,)))
        gp[...] += x.astype(F32) * rrow[pl.ds(g, 1), :]

    def add_y(g):
        acc[1] += mm(gx[1, g], w2v[:, block_at(g)], ((1,), (1,)))

    def use(a, y_):
        @pl.loop(0, 2)
        def _(k):
            g = 4 * y_ + 2 * c + k
            o = 4 * y_ + 2 * (1 - c) + k
            (add_x, add_y)[a](g)
            arrived(gx.at[a, o], agr.at[a, o, 0])
            (add_x, add_y)[a](o)

    compact(0)
    fan(0, y, h, Z)
    fan(0, y, h, N)
    fan(0, y, h, B)
    fan(0, y, h, C)
    compact(1)
    fan(1, y, h, N)
    fan(1, y, h, B)
    fan(1, y, h, Z)
    fan(1, y, h, C)
    loads[2].wait()
    loads[3].wait()
    got(0, y, 1 - h)
    fan(0, y, 1 - h, N)
    fan(0, y, 1 - h, B)
    fan(0, y, 1 - h, C)
    got(0, yp, h)
    fan(0, yp, h, N, 0)
    fan(0, yp, h, C)
    got(0, yn, h)
    fan(0, yn, h, B, 1)
    fan(0, yn, h, C)
    got(1, yp, h)
    fan(1, yp, h, N, 0)
    fan(1, yp, h, Z)
    fan(1, yp, h, C)
    got(1, yn, h)
    fan(1, yn, h, B, 1)
    fan(1, yn, h, Z)
    fan(1, yn, h, C)
    use(0, y)
    got(0, yp, 1 - h)
    fan(0, yp, 1 - h, N, 0)
    fan(0, yp, 1 - h, C)
    got(0, yn, 1 - h)
    fan(0, yn, 1 - h, B, 1)
    fan(0, yn, 1 - h, C)
    got_halves(0, yo, h)
    fan(0, yo, h, C)
    got_halves(1, yo, h)
    fan(1, yo, h, Z)
    fan(1, yo, h, C)
    use(0, yp)
    use(0, yn)
    got_halves(0, yo, 1 - h)
    fan(0, yo, 1 - h, C)
    got(1, y, 1 - h)
    fan(1, y, 1 - h, C)
    use(0, yo)
    use(1, y)
    got(1, yp, 1 - h)
    fan(1, yp, 1 - h, C)
    got(1, yn, 1 - h)
    fan(1, yn, 1 - h, C)
    use(1, yp)
    got(1, yo, 1 - h)
    fan(1, yo, 1 - h, C)
    use(1, yn)
    use(1, yo)

    er_rows = 64

    @pl.loop(0, cap // er_rows)
    def _(i):
        at = pl.ds(pl.multiple_of(i * er_rows, er_rows), er_rows)
        gate = jax.nn.sigmoid(jnp.sum(gp[at, :], axis=1, keepdims=True))
        pre = acc[0, at, :]
        up = acc[1, at, :]
        sig = jax.nn.sigmoid(pre)
        hidden = pre * sig
        hg[at, :] = (gate * hidden).astype(BF)
        gate_grad = jnp.sum(hidden * up, axis=1, keepdims=True)
        da[at, :] = (gate * up * sig * (1.0 + pre * (1.0 - sig))).astype(BF)
        score = gate_grad * gate * (1.0 - gate)
        dsb[at, :] = jnp.broadcast_to(score, (er_rows, dsb.shape[1]))

    def r_block(g):
        s = dsb[...]
        wide = jnp.concatenate([s, s], axis=1)
        rb[g] = (mm(da[...], w1v[block_at(g), :], ((1,), (1,))) + wide * rrow[pl.ds(g, 1), :]).astype(BF)

    @pl.loop(0, groups // 2)
    def _(j):
        g = 4 * (j // 2) + 2 * (1 - c) + j % 2
        r_block(g)
        rcopy(rb.at[g], cb.at[j], cs.at[j], cr.at[j], cdev).start()

    s = dsb[...]
    s_hi = s.astype(BF).astype(F32)
    s_mid = (s - s_hi).astype(BF).astype(F32)
    s_lo = s - s_hi - s_mid
    lane = lax.broadcasted_iota(jnp.int32, s.shape, 1)
    terms = jnp.where(lane == 0, s_hi, jnp.where(lane == 1, s_mid, jnp.where(lane == 2, s_lo, 0.0)))
    terms = jnp.transpose(terms)[:16].astype(BF)

    @pl.loop(0, groups)
    def _(g):
        rp[g // 2, g % 2] = mm(terms, gx[0, g], ((1,), (0,)))[:8]

    @pl.loop(1, nt)
    def _(d):
        to = (t + d) % nt
        rcopy(rp.at[to], rq.at[t], r1s.at[to], r1r.at[t], (me, to)).start()

    @pl.loop(0, groups // 2)
    def _(j):
        g = 4 * (j // 2) + 2 * c + j % 2
        r_block(g)

    @pl.loop(0, groups // 2)
    def _(j):
        g = 4 * (j // 2) + 2 * c + j % 2
        arrived(cb.at[j], cr.at[j])
        cb[j] = (cb[j].astype(F32) + rb[g].astype(F32)).astype(BF)

    low = pl.ds(0, half)
    high = pl.ds(half, half)
    for k in range(RING):
        send(cb.at[2 * k + 1 - h, low], zb.at[k], zzs.at[k], zzr.at[k], zdev)
    for k in range(2):
        send(cb.at[2 * yo + k, pl.ds(half, quarter)], yi.at[k, 0], yis.at[k, 0], yir.at[k, 0], ynd)
        send(cb.at[2 * yo + k, pl.ds(half + quarter, quarter)], yi.at[k, 1], yis.at[k, 1], yir.at[k, 1], ypd)

    def weight_grads(first, count):
        @pl.loop(first, first + count)
        def _(g):
            goutv[:, block_at(g)] = mm(hg[...], gx[1, g], ((0,), (0,))).astype(BF)
            ginv[block_at(g), :] = mm(gx[0, g], da[...], ((0,), (0,))).astype(BF)

    @pl.loop(1, nt)
    def _(d):
        source = (t + nt - d) % nt
        arrived(rq.at[source], r1r.at[source])

    rq[t] = rp[t]
    total = rq[0]
    for k in range(1, nt):
        total = total + rq[k]
    rs1[...] = total
    send(rs1.at[1 - h], rz, rzs, rzr, zdev)

    weight_grads(0, 3)
    for k in range(2):
        arrived(yi.at[k, 0], yir.at[k, 0])
        arrived(yi.at[k, 1], yir.at[k, 1])
        first = pl.ds(half, quarter)
        second = pl.ds(half + quarter, quarter)
        cb[2 * yn + k, first] = (cb[2 * yn + k, first].astype(F32) + yi[k, 0].astype(F32)).astype(BF)
        cb[2 * yp + k, second] = (cb[2 * yp + k, second].astype(F32) + yi[k, 1].astype(F32)).astype(BF)
        send(cb.at[2 * yn + k, high], yj.at[k, 0], yjs.at[k, 0], yjr.at[k, 0], ynd)
        send(cb.at[2 * yp + k, high], yj.at[k, 1], yjs.at[k, 1], yjr.at[k, 1], ypd)

    arrived(rz, rzr)
    col = jnp.sum(rs1[h] + rz[...], axis=0, keepdims=True)
    rv[...] = jnp.broadcast_to(col, rv.shape)
    rw[me] = jnp.broadcast_to(col, rv.shape)

    @pl.loop(1, ne)
    def _(d):
        to = (me + d) % ne
        rcopy(rv, rw.at[me], r2s.at[to], r2r.at[me], (to, t)).start()

    weight_grads(3, 4)
    for k in range(RING):
        arrived(zb.at[k], zzr.at[k])

        @pl.when(k != y)
        def _():
            zb[k] = (zb[k].astype(F32) + cb[2 * k + h, low].astype(F32)).astype(BF)

    send(zb.at[yo, pl.ds(0, quarter)], yk.at[0], yks.at[0], ykr.at[0], ynd)
    send(zb.at[yo, pl.ds(quarter, quarter)], yk.at[1], yks.at[1], ykr.at[1], ypd)

    weight_grads(7, 3)
    base = 2 * y + 1 - h
    for k in range(2):
        for side in range(2):
            arrived(yj.at[k, side], yjr.at[k, side])
    cb[base, high] = (
        cb[base, high].astype(F32) + (yj[1 - h, 0].astype(F32) + yj[1 - h, 1].astype(F32))
    ).astype(BF)
    send(cb.at[base, high], zf, zfs, zfr, zdev)
    for side in range(2):
        arrived(yk.at[side], ykr.at[side])
    first = pl.ds(0, quarter)
    second = pl.ds(quarter, quarter)
    zb[yn, first] = (zb[yn, first].astype(F32) + yk[0].astype(F32)).astype(BF)
    zb[yp, second] = (zb[yp, second].astype(F32) + yk[1].astype(F32)).astype(BF)
    send(zb.at[yn], yl.at[0], yls.at[0], ylr.at[0], ynd)
    send(zb.at[yp], yl.at[1], yls.at[1], ylr.at[1], ypd)

    @pl.loop(1, ne)
    def _(d):
        source = (me + ne - d) % ne
        arrived(rw.at[source], r2r.at[source])

    for k in range(ne):
        rxs[k // 2:k // 2 + 1, (k % 2) * share:(k % 2 + 1) * share] = rw[k, 0:1, :]
    ry[t] = rxs[...]

    @pl.loop(1, nt)
    def _(d):
        to = (t + d) % nt
        rcopy(rxs, ry.at[t], r3s.at[to], r3r.at[t], (me, to)).start()

    weight_grads(10, 6)
    out_copies = [
        pltpu.make_async_copy(ginv, gin, outs.at[0]),
        pltpu.make_async_copy(goutv, gout, outs.at[1]),
    ]
    for copy in out_copies:
        copy.start()

    mine = 2 * y + h
    arrived(zf, zfr)
    fb[high, :] = (
        cb[mine, high].astype(F32) + (yj[h, 0].astype(F32) + yj[h, 1].astype(F32)) + zf[...].astype(F32)
    ).astype(BF)
    for side in range(2):
        arrived(yl.at[side], ylr.at[side])
    fb[low, :] = (
        cb[mine, low].astype(F32) + zb[y].astype(F32) + (yl[0].astype(F32) + yl[1].astype(F32))
    ).astype(BF)

    @pl.loop(0, ne * bucket // rows)
    def _(i):
        spread = (
            lax.broadcasted_iota(jnp.int32, (rows, cap), 0) + i * rows == q_row[...]
        ).astype(BF)
        es[pl.ds(i * (rows // bucket), rows // bucket)] = (
            mm(spread, fb[...], ((1,), (0,))).astype(BF).reshape(rows // bucket, bucket, share)
        )

    @pl.loop(1, ne)
    def _(d):
        to = (me + d) % ne
        rcopy(es.at[to], er.at[me // 2, h], rets.at[to], retr.at[me], (to, t)).start()

    er[me // 2, h] = es[me]

    @pl.loop(1, nt)
    def _(d):
        source = (t + nt - d) % nt
        arrived(ry.at[source], r3r.at[source])

    for k in range(nt):
        gr[:, k * feat:(k + 1) * feat] = ry[k]

    @pl.loop(1, ne)
    def _(d):
        source = (me + ne - d) % ne
        arrived(er.at[source // 2, source % 2], retr.at[source])

    home = (lax.broadcasted_iota(jnp.int32, (gt.shape[0], slots), 0) == sel_row[...]).astype(BF)
    for k in range(2):
        gt[:, k * share:(k + 1) * share] = mm(home, er[:, k].reshape(slots, share), ((1,), (0,))).astype(BF)

    @pl.loop(1, ne)
    def _(d):
        to = (me + d) % ne
        for a in range(2):
            rcopy(sx.at[a, 0, 0], rx.at[a, 0], p1s.at[a, to], p1r.at[a, to], zdev).wait_send()
        rcopy(rv, rw.at[0], r2s.at[to], r2r.at[to], zdev).wait_send()
        rcopy(es.at[0], er.at[0, 0], rets.at[to], retr.at[to], zdev).wait_send()

    @pl.loop(1, nt)
    def _(d):
        to = (t + d) % nt
        rcopy(rp.at[0], rq.at[0], r1s.at[to], r1r.at[to], zdev).wait_send()
        rcopy(rxs, ry.at[0], r3s.at[to], r3r.at[to], zdev).wait_send()

    @pl.loop(0, groups // 2)
    def _(j):
        rcopy(rb.at[j], cb.at[j], cs.at[j], cr.at[j], zdev).wait_send()

    for copy in pending:
        copy.wait_send()
    for copy in out_copies:
        copy.wait()


def body(tokens, cotangent, w_in, w_out, router, chosen):
    tok_dev, features = tokens.shape
    hidden = w_in.shape[1]
    ne = lax.axis_size("expert")
    nt = lax.axis_size("tensor")
    bucket = 4 * tok_dev // ne
    experts, cap = chosen.shape
    me = lax.axis_index("expert")
    expert = me // 2
    first = me * tok_dev
    feat = features // nt
    share = feat // 2
    groups = features // share

    starts = jnp.sum((chosen < first).astype(jnp.int32), axis=1)
    place = jnp.arange(cap, dtype=jnp.int32)
    slot = jnp.arange(bucket, dtype=jnp.int32)
    want = starts[:, None] + slot[None, :]
    sel = jnp.sum(
        jnp.where(place[None, None, :] == want[:, :, None], chosen[:, None, :] + 1, 0), axis=2
    ) - 1 - first
    sel = sel.reshape(experts * bucket)
    mine = lax.dynamic_index_in_dim(chosen, expert, 0, keepdims=False)
    home = mine // tok_dev
    before = jnp.sum((mine[None, :] < (home * tok_dev)[:, None]).astype(jnp.int32), axis=1)
    q = home * bucket + place - before
    rrow = lax.dynamic_index_in_dim(router, expert, 1, keepdims=False).astype(F32).reshape(groups, share)

    vm = lambda shape, kind: pltpu.VMEM(shape, kind)
    dma = lambda *shape: pltpu.SemaphoreType.DMA(shape)
    vspec = pl.BlockSpec(memory_space=pltpu.VMEM)
    aspec = pl.BlockSpec(memory_space=pl.ANY)
    half, quarter = cap // 2, cap // 4
    g2 = groups // 2
    scratch = [
        vm((2, tok_dev, feat), BF),
        vm((features, hidden), BF),
        vm((hidden, features), BF),
        vm((2, experts, 2, bucket, share), BF),
        vm((2, ne, bucket, share), BF),
        vm((2, groups, cap, share), BF),
        vm((2, cap, hidden), F32),
        vm((cap, share), F32),
        vm((cap, hidden), BF),
        vm((cap, hidden), BF),
        vm((cap, 128), F32),
        vm((groups, cap, share), BF),
        vm((g2, cap, share), BF),
        vm((RING, half, share), BF),
        vm((2, 2, quarter, share), BF),
        vm((2, 2, half, share), BF),
        vm((2, quarter, share), BF),
        vm((2, half, share), BF),
        vm((half, share), BF),
        vm((8, 128), F32),
        vm((cap, share), BF),
        vm((ne, bucket, share), BF),
        vm((experts, 2, bucket, share), BF),
        vm((features, hidden), BF),
        vm((hidden, features), BF),
        vm((nt, 2, 8, share), F32),
        vm((nt, 2, 8, share), F32),
        vm((2, 8, share), F32),
        vm((8, share), F32),
        vm((8, share), F32),
        vm((ne, 8, share), F32),
        vm((experts, feat), F32),
        vm((nt, experts, feat), F32),
        dma(4), dma(2, ne), dma(2, ne), dma(2, g2, 2, 4), dma(2, groups, 2),
        dma(g2), dma(g2), dma(RING), dma(RING), dma(2, 2), dma(2, 2), dma(2, 2), dma(2, 2),
        dma(2), dma(2), dma(2), dma(2), pltpu.SemaphoreType.DMA, pltpu.SemaphoreType.DMA,
        dma(ne), dma(ne), dma(nt), dma(nt), pltpu.SemaphoreType.DMA, pltpu.SemaphoreType.DMA,
        dma(ne), dma(ne), dma(nt), dma(nt), dma(2),
    ]
    gt, gin, gout, gr = pl.pallas_call(
        functools.partial(step_kernel, ne, nt, bucket),
        out_shape=(
            jax.ShapeDtypeStruct((tok_dev, feat), BF),
            jax.ShapeDtypeStruct((features, hidden), BF),
            jax.ShapeDtypeStruct((hidden, features), BF),
            jax.ShapeDtypeStruct((experts, features), F32),
        ),
        in_specs=[aspec, aspec, aspec, aspec, vspec, vspec, vspec, vspec, vspec],
        out_specs=(vspec, aspec, aspec, vspec),
        scratch_shapes=scratch,
        compiler_params=pltpu.CompilerParams(
            collective_id=0, has_side_effects=True, vmem_limit_bytes=60 * 1024 * 1024
        ),
        name="moe_step",
    )(
        tokens, cotangent, w_in, w_out, rrow,
        sel.reshape(-1, 1), sel.reshape(1, -1), q.reshape(-1, 1), q.reshape(1, -1),
    )
    return gt, gin, gout, gr.T


def solution(mesh):
    placed = (
        P("expert", None),
        P("expert", None),
        P(None, ("expert", "tensor")),
        P(("expert", "tensor"), None),
        P(),
        P(),
    )
    return jax.shard_map(
        body,
        mesh=mesh,
        in_specs=placed,
        out_specs=(
            P("expert", "tensor"),
            P(None, ("expert", "tensor")),
            P(("expert", "tensor"), None),
            P(),
        ),
        check_vma=False,
    )
```

```python
import functools

import jax
import jax.numpy as jnp
from jax import lax
from jax.experimental import pallas as pl
from jax.experimental.pallas import tpu as pltpu
from jax.sharding import PartitionSpec as P

MESH = pl.DeviceIdType.MESH
BF = jnp.bfloat16
F32 = jnp.float32
RING = 4


def mm(a, b, dims):
    return lax.dot_general(a, b, (dims, ((), ())), preferred_element_type=F32)


def step_kernel(
    ne, nt, bucket,
    tok, cot, w_in, w_out, rt, chosen,
    gt, gin, gout, gr,
    chf, rrow, hot, q_row, q_col,
    tv, w1v, w2v, sx, rx, gx, acc, gp, hg, da, dsb, rb, cb, zb, yi, yj, yk, yl, zf, fv, fb, es, er,
    ginv, goutv, rp, rq, rs1, rz, rv, rw, rxs, ry,
    ld, p1s, p1r, fws, pcs, pcr, ags, agr, cs, cr, zzs, zzr, yis, yir, yjs, yjr, yks, ykr, yls, ylr, zfs, zfr,
    rets, retr, r1s, r1r, rzs, rzr, r2s, r2r, r3s, r3r, outs,
):
    me = lax.axis_index("expert")
    t = lax.axis_index("tensor")
    h = me % 2
    y = t // 2
    c = t % 2
    feat = tv.shape[2]
    share = feat // 2
    cap = hg.shape[0]
    groups = gx.shape[1]
    half = cap // 2
    quarter = cap // 4

    zdev = (me + 1 - 2 * h, t)
    cdev = (me, 2 * y + 1 - c)
    yn = (y + 1) % RING
    yp = (y + 3) % RING
    yo = (y + 2) % RING
    ynd = (me, 2 * yn + c)
    ypd = (me, 2 * yp + c)

    def rcopy(src, dst, ss, rs, dev):
        return pltpu.make_async_remote_copy(
            src_ref=src, dst_ref=dst, send_sem=ss, recv_sem=rs, device_id=dev, device_id_type=MESH
        )

    pending = []

    def send(src, dst, ss, rs, dev):
        copy = rcopy(src, dst, ss, rs, dev)
        copy.start()
        pending.append(copy)

    def arrived(dst, rs):
        rcopy(dst, dst, rs, rs, zdev).wait_recv()

    loads = [
        pltpu.make_async_copy(tok.at[:, pl.ds(pl.multiple_of(t * feat, feat), feat)], tv.at[0], ld.at[0]),
        pltpu.make_async_copy(cot.at[:, pl.ds(pl.multiple_of(t * feat, feat), feat)], tv.at[1], ld.at[1]),
        pltpu.make_async_copy(w_in, w1v, ld.at[2]),
        pltpu.make_async_copy(w_out, w2v, ld.at[3]),
    ]
    for load in loads:
        load.start()

    barrier = pltpu.get_barrier_semaphore()

    @pl.loop(1, ne)
    def _(d):
        pl.semaphore_signal(barrier, inc=1, device_id=((me + d) % ne, t), device_id_type=MESH)

    @pl.loop(1, nt)
    def _(d):
        pl.semaphore_signal(barrier, inc=1, device_id=(me, (t + d) % nt), device_id_type=MESH)

    experts = chosen.shape[0]
    tok_dev = tv.shape[1]
    slots = experts * bucket
    zr = ne // RING
    x = me // zr
    z = me % zr
    first = (me * tok_dev).astype(F32)
    chf[...] = chosen[...].astype(F32)
    col = lax.broadcasted_iota(jnp.int32, (bucket, cap), 1).astype(F32)
    row = lax.broadcasted_iota(jnp.int32, (bucket, cap), 0).astype(F32)
    tok_at = lax.broadcasted_iota(jnp.int32, (bucket, tok_dev), 1).astype(F32)

    @pl.loop(0, experts)
    def _(k):
        picks = chf[pl.ds(k, 1), :]
        start = jnp.sum(jnp.where(picks < first, 1.0, 0.0), axis=1, keepdims=True)
        held = jnp.sum(jnp.where(col == row + start, picks + 1.0, 0.0), axis=1, keepdims=True) - 1.0 - first
        hot[pl.ds(pl.multiple_of(k * bucket, bucket), bucket), :] = jnp.where(tok_at == held, 1.0, 0.0).astype(BF)

    for a in range(2):
        loads[a].wait()
        for k in range(2):
            packed = mm(hot[...], tv[a, :, k * share:(k + 1) * share], ((1,), (0,))).astype(BF)
            sx[a, :, k] = packed.reshape(slots // bucket, bucket, share)
        if a == 0:
            pl.semaphore_wait(barrier, ne + nt - 2)

        @pl.loop(0, experts)
        def _(k):
            target = (x * (zr // 2) + z // 2 + k) % experts
            near = ((2 * target) % zr + zr - z) % zr // (zr // 2)
            to = 2 * target + near

            @pl.when(to != me)
            def _():
                rcopy(sx.at[a, target], rx.at[a, me], p1s.at[a, target], p1r.at[a, me], (to, t)).start()

            @pl.when(to == me)
            def _():
                rx[a, me] = sx[a, target]

    home_row = lax.broadcasted_iota(jnp.int32, (ne, cap), 0).astype(F32)
    place = lax.broadcasted_iota(jnp.int32, (ne, cap), 1).astype(F32)
    mine_row = chf[pl.ds(me // 2, 1), :]
    low_bound = home_row * float(tok_dev)
    before = jnp.sum(jnp.where(mine_row < low_bound, 1.0, 0.0), axis=1, keepdims=True)
    inside = jnp.logical_and(mine_row >= low_bound, mine_row < low_bound + float(tok_dev))
    q = jnp.sum(jnp.where(inside, home_row * float(bucket) + place - before, 0.0), axis=0, keepdims=True)
    q_row[...] = jnp.broadcast_to(q, q_row.shape)
    q_col[...] = jnp.transpose(jnp.broadcast_to(q, (128, cap)))
    router_all = rt[...].astype(F32)
    rrow[...] = jnp.broadcast_to(
        jnp.sum(
            jnp.where(lax.broadcasted_iota(jnp.int32, router_all.shape, 0) == me // 2, router_all, 0.0),
            axis=0, keepdims=True,
        ),
        rrow.shape,
    )

    own_g = 4 * y + 2 * c + h

    def fan(a, y_, h_, target, part=None):
        g = 4 * y_ + 2 * c + h_
        j = 2 * y_ + h_
        dev = (zdev, ynd, ypd, cdev)[target]
        if part is None:
            ref = gx.at[a, g]
            send(ref, ref, ags.at[a, j, 0, target], agr.at[a, g, 0], dev)
        else:
            ref = gx.at[a, g, pl.ds(part * half, half)]
            send(ref, ref, ags.at[a, j, part, target], agr.at[a, g, part], dev)

    def got(a, y_, h_):
        g = 4 * y_ + 2 * c + h_
        arrived(gx.at[a, g], agr.at[a, g, 0])

    def got_halves(a, y_, h_):
        g = 4 * y_ + 2 * c + h_
        for part in range(2):
            arrived(gx.at[a, g, pl.ds(part * half, half)], agr.at[a, g, part])

    Z, N, B, C = 0, 1, 2, 3
    rows = 128

    buckets = ne * bucket
    zdir = 1 - 2 * h

    def near_home(i, toward):
        zz = (z + zr + toward * (i // RING) + (toward + zdir) // 2) % zr
        return ((x + i) % RING) * zr + zz

    def near_rows(a, first_i, count):
        @pl.loop(first_i, first_i + count)
        def _(i):
            source = near_home(i, -zdir)

            @pl.when(source != me)
            def _():
                arrived(rx.at[a, source], p1r.at[a, source])

            ref = rx.at[a, source, 1 - h]
            rcopy(ref, ref, fws.at[a, source], p1r.at[a, source], zdev).start()

    def far_rows(a):
        @pl.loop(0, ne // 2)
        def _(i):
            source = near_home(i, zdir)
            arrived(rx.at[a, source, h], p1r.at[a, source])

    def compact(a):
        @pl.loop(0, cap // rows)
        def _(i):
            at = pl.ds(pl.multiple_of(i * rows, rows), rows)
            slot = lax.broadcasted_iota(jnp.int32, (rows, buckets), 1).astype(F32)
            pick = jnp.where(slot == q_col[at, 0:1], 1.0, 0.0).astype(BF)
            gx[a, own_g, at] = mm(pick, rx[a, :, h].reshape(buckets, share), ((1,), (0,))).astype(BF)

    acc[...] = jnp.zeros_like(acc)
    gp[...] = jnp.zeros_like(gp)

    def block_at(g):
        return pl.ds(pl.multiple_of(g * share, share), share)

    def add_x(g):
        x = gx[0, g]
        acc[0] += mm(x, w1v[block_at(g), :], ((1,), (0,)))
        gp[...] += x.astype(F32) * rrow[0:1, block_at(g)]

    def add_y(g):
        acc[1] += mm(gx[1, g], w2v[:, block_at(g)], ((1,), (1,)))

    def use(a, y_):
        @pl.loop(0, 2)
        def _(k):
            g = 4 * y_ + 2 * c + k
            o = 4 * y_ + 2 * (1 - c) + k
            (add_x, add_y)[a](g)
            arrived(gx.at[a, o], agr.at[a, o, 0])
            (add_x, add_y)[a](o)

    def got_half(a, y_, h_, part):
        g = 4 * y_ + 2 * c + h_
        arrived(gx.at[a, g, pl.ds(part * half, half)], agr.at[a, g, part])

    near_rows(0, 0, ne // 2)
    far_rows(0)
    compact(0)
    fan(0, y, h, N)
    fan(0, y, h, B)
    fan(0, y, h, Z)
    fan(0, y, h, C)
    near_rows(1, 0, ne // 4)
    got(0, y, 1 - h)
    fan(0, y, 1 - h, N)
    fan(0, y, 1 - h, B)
    fan(0, y, 1 - h, C)
    got(0, yp, h)
    fan(0, yp, h, N, 0)
    fan(0, yp, h, C)
    got(0, yn, h)
    fan(0, yn, h, B, 1)
    fan(0, yn, h, C)
    near_rows(1, ne // 4, ne // 4)
    loads[2].wait()
    use(0, y)
    far_rows(1)
    compact(1)
    fan(1, y, h, Z, 1)
    fan(1, y, h, N, 0)
    fan(1, y, h, B, 0)
    fan(1, y, h, N, 1)
    fan(1, y, h, B, 1)
    fan(1, y, h, Z, 0)
    fan(1, y, h, C)
    got(0, yp, 1 - h)
    fan(0, yp, 1 - h, N, 0)
    fan(0, yp, 1 - h, C)
    got(0, yn, 1 - h)
    fan(0, yn, 1 - h, B, 1)
    fan(0, yn, 1 - h, C)
    got_halves(0, yo, h)
    fan(0, yo, h, C)
    use(0, yp)
    got_half(1, y, 1 - h, 1)
    fan(1, y, 1 - h, N, 1)
    fan(1, y, 1 - h, B, 1)
    loads[3].wait()
    eighth = half // 2

    def piece(a, y_, h_, part, k):
        g = 4 * y_ + 2 * c + h_
        return gx.at[a, g, pl.ds(part * half + k * eighth, eighth)]

    def relay(y_, h_, part, k, target):
        g = 4 * y_ + 2 * c + h_
        ref = piece(1, y_, h_, part, k)
        send(ref, ref, pcs.at[h_, part, k], pcr.at[h_, part, k], (zdev, ynd, ypd, cdev)[target])

    def got_pieces(y_, h_, part):
        for k in range(2):
            arrived(piece(1, y_, h_, part, k), pcr.at[h_, part, k])

    got_half(1, yp, h, 0)
    relay(yp, h, 0, 0, N)
    fan(1, yp, h, Z, 0)
    got_half(1, yn, h, 0)
    relay(yn, h, 0, 1, B)
    fan(1, yn, h, Z, 0)
    got_halves(0, yo, 1 - h)
    fan(0, yo, 1 - h, C)
    use(0, yn)
    got_half(1, yp, h, 1)
    relay(yp, h, 1, 0, N)
    fan(1, yp, h, C)
    got_half(1, yn, h, 1)
    relay(yn, h, 1, 1, B)
    fan(1, yn, h, C)
    got_half(1, y, 1 - h, 0)
    fan(1, y, 1 - h, C)
    use(0, yo)
    got_pieces(yo, h, 0)
    fan(1, yo, h, Z, 0)
    got_half(1, yp, 1 - h, 1)
    relay(yp, 1 - h, 1, 0, N)
    got_half(1, yn, 1 - h, 1)
    relay(yn, 1 - h, 1, 1, B)
    use(1, y)
    got_half(1, yp, 1 - h, 0)
    fan(1, yp, 1 - h, C)
    got_half(1, yn, 1 - h, 0)
    fan(1, yn, 1 - h, C)
    got_pieces(yo, h, 1)
    fan(1, yo, h, C)
    use(1, yp)
    got_half(1, yo, 1 - h, 0)
    got_pieces(yo, 1 - h, 1)
    fan(1, yo, 1 - h, C)
    use(1, yn)
    use(1, yo)

    er_rows = 64

    @pl.loop(0, cap // er_rows)
    def _(i):
        at = pl.ds(pl.multiple_of(i * er_rows, er_rows), er_rows)
        gate = jax.nn.sigmoid(jnp.sum(gp[at, :], axis=1, keepdims=True))
        pre = acc[0, at, :]
        up = acc[1, at, :]
        sig = jax.nn.sigmoid(pre)
        hidden = pre * sig
        hg[at, :] = (gate * hidden).astype(BF)
        gate_grad = jnp.sum(hidden * up, axis=1, keepdims=True)
        da[at, :] = (gate * up * sig * (1.0 + pre * (1.0 - sig))).astype(BF)
        score = gate_grad * gate * (1.0 - gate)
        dsb[at, :] = jnp.broadcast_to(score, (er_rows, dsb.shape[1]))

    def r_value(g):
        s = dsb[...]
        wide = jnp.concatenate([s, s], axis=1)
        return mm(da[...], w1v[block_at(g), :], ((1,), (1,))) + wide * rrow[0:1, block_at(g)]

    @pl.loop(0, groups // 2)
    def _(j):
        place_y = (yo + j // 2) % RING
        i = 2 * place_y + j % 2
        rb[i] = r_value(4 * place_y + 2 * (1 - c) + j % 2).astype(BF)
        rcopy(rb.at[i], cb.at[i], cs.at[i], cr.at[i], cdev).start()

    s = dsb[...]
    s_hi = s.astype(BF).astype(F32)
    s_mid = (s - s_hi).astype(BF).astype(F32)
    s_lo = s - s_hi - s_mid
    lane = lax.broadcasted_iota(jnp.int32, s.shape, 1)
    terms = jnp.where(lane == 0, s_hi, jnp.where(lane == 1, s_mid, jnp.where(lane == 2, s_lo, 0.0)))
    terms = jnp.transpose(terms)[:16].astype(BF)

    @pl.loop(0, groups)
    def _(g):
        rp[g // 2, g % 2] = mm(terms, gx[0, g], ((1,), (0,)))[:8]

    @pl.loop(1, nt)
    def _(d):
        to = (t + d) % nt
        rcopy(rp.at[to], rq.at[t], r1s.at[to], r1r.at[t], (me, to)).start()

    low = pl.ds(0, half)
    high = pl.ds(half, half)
    for place_y in (yo, yp, y, yn):
        @pl.loop(0, 2)
        def _(k):
            j = 2 * place_y + k
            value = r_value(4 * place_y + 2 * c + k)
            arrived(cb.at[j], cr.at[j])
            cb[j] = (cb[j].astype(F32) + value).astype(BF)

        if place_y is yo:
            for k in range(2):
                send(cb.at[2 * yo + k, pl.ds(half, quarter)], yi.at[k, 0], yis.at[k, 0], yir.at[k, 0], ynd)
                send(cb.at[2 * yo + k, pl.ds(half + quarter, quarter)], yi.at[k, 1], yis.at[k, 1], yir.at[k, 1], ypd)
        send(cb.at[2 * place_y + 1 - h, low], zb.at[place_y], zzs.at[place_y], zzr.at[place_y], zdev)

    def weight_grads(first, count):
        @pl.loop(first, first + count)
        def _(g):
            goutv[:, block_at(g)] = mm(hg[...], gx[1, g], ((0,), (0,))).astype(BF)
            ginv[block_at(g), :] = mm(gx[0, g], da[...], ((0,), (0,))).astype(BF)

    @pl.loop(1, nt)
    def _(d):
        source = (t + nt - d) % nt
        arrived(rq.at[source], r1r.at[source])

    rq[t] = rp[t]
    total = rq[0]
    for k in range(1, nt):
        total = total + rq[k]
    rs1[...] = total
    send(rs1.at[1 - h], rz, rzs, rzr, zdev)

    weight_grads(0, 3)
    for k in range(2):
        arrived(yi.at[k, 0], yir.at[k, 0])
        arrived(yi.at[k, 1], yir.at[k, 1])
        first = pl.ds(half, quarter)
        second = pl.ds(half + quarter, quarter)
        cb[2 * yn + k, first] = (cb[2 * yn + k, first].astype(F32) + yi[k, 0].astype(F32)).astype(BF)
        cb[2 * yp + k, second] = (cb[2 * yp + k, second].astype(F32) + yi[k, 1].astype(F32)).astype(BF)
        send(cb.at[2 * yn + k, high], yj.at[k, 0], yjs.at[k, 0], yjr.at[k, 0], ynd)
        send(cb.at[2 * yp + k, high], yj.at[k, 1], yjs.at[k, 1], yjr.at[k, 1], ypd)

    arrived(rz, rzr)
    col = jnp.sum(rs1[h] + rz[...], axis=0, keepdims=True)
    rv[...] = jnp.broadcast_to(col, rv.shape)
    rw[me] = jnp.broadcast_to(col, rv.shape)

    @pl.loop(1, ne)
    def _(d):
        to = (me + d) % ne
        rcopy(rv, rw.at[me], r2s.at[to], r2r.at[me], (to, t)).start()

    weight_grads(3, 4)
    for k in range(RING):
        arrived(zb.at[k], zzr.at[k])

        @pl.when(k != y)
        def _():
            zb[k] = (zb[k].astype(F32) + cb[2 * k + h, low].astype(F32)).astype(BF)

    send(zb.at[yo, pl.ds(0, quarter)], yk.at[0], yks.at[0], ykr.at[0], ynd)
    send(zb.at[yo, pl.ds(quarter, quarter)], yk.at[1], yks.at[1], ykr.at[1], ypd)

    weight_grads(7, 3)
    base = 2 * y + 1 - h
    for k in range(2):
        for side in range(2):
            arrived(yj.at[k, side], yjr.at[k, side])
    cb[base, high] = (
        cb[base, high].astype(F32) + (yj[1 - h, 0].astype(F32) + yj[1 - h, 1].astype(F32))
    ).astype(BF)
    send(cb.at[base, high], zf, zfs, zfr, zdev)
    for side in range(2):
        arrived(yk.at[side], ykr.at[side])
    first = pl.ds(0, quarter)
    second = pl.ds(quarter, quarter)
    zb[yn, first] = (zb[yn, first].astype(F32) + yk[0].astype(F32)).astype(BF)
    zb[yp, second] = (zb[yp, second].astype(F32) + yk[1].astype(F32)).astype(BF)
    send(zb.at[yn], yl.at[0], yls.at[0], ylr.at[0], ynd)
    send(zb.at[yp], yl.at[1], yls.at[1], ylr.at[1], ypd)

    @pl.loop(1, ne)
    def _(d):
        source = (me + ne - d) % ne
        arrived(rw.at[source], r2r.at[source])

    for k in range(ne):
        rxs[k // 2:k // 2 + 1, (k % 2) * share:(k % 2 + 1) * share] = rw[k, 0:1, :]
    ry[t] = rxs[...]

    @pl.loop(1, nt)
    def _(d):
        to = (t + d) % nt
        rcopy(rxs, ry.at[t], r3s.at[to], r3r.at[t], (me, to)).start()

    weight_grads(10, 6)
    out_copies = [
        pltpu.make_async_copy(ginv, gin, outs.at[0]),
        pltpu.make_async_copy(goutv, gout, outs.at[1]),
    ]
    for copy in out_copies:
        copy.start()

    mine = 2 * y + h
    arrived(zf, zfr)
    fb[high, :] = (
        cb[mine, high].astype(F32) + (yj[h, 0].astype(F32) + yj[h, 1].astype(F32)) + zf[...].astype(F32)
    ).astype(BF)
    for side in range(2):
        arrived(yl.at[side], ylr.at[side])
    fb[low, :] = (
        cb[mine, low].astype(F32) + zb[y].astype(F32) + (yl[0].astype(F32) + yl[1].astype(F32))
    ).astype(BF)

    @pl.loop(0, ne * bucket // rows)
    def _(i):
        spread = (
            (lax.broadcasted_iota(jnp.int32, (rows, cap), 0) + i * rows).astype(F32) == q_row[0:1, :]
        ).astype(BF)
        es[pl.ds(i * (rows // bucket), rows // bucket)] = (
            mm(spread, fb[...], ((1,), (0,))).astype(BF).reshape(rows // bucket, bucket, share)
        )

    @pl.loop(1, ne)
    def _(d):
        to = (me + d) % ne
        rcopy(es.at[to], er.at[me // 2, h], rets.at[to], retr.at[me], (to, t)).start()

    er[me // 2, h] = es[me]

    @pl.loop(1, nt)
    def _(d):
        source = (t + nt - d) % nt
        arrived(ry.at[source], r3r.at[source])

    for k in range(nt):
        gr[:, k * feat:(k + 1) * feat] = ry[k]

    @pl.loop(1, ne)
    def _(d):
        source = (me + ne - d) % ne
        arrived(er.at[source // 2, source % 2], retr.at[source])

    for k in range(2):
        gt[:, k * share:(k + 1) * share] = mm(hot[...], er[:, k].reshape(slots, share), ((0,), (0,))).astype(BF)

    @pl.loop(1, ne)
    def _(d):
        to = (me + d) % ne
        rcopy(rv, rw.at[0], r2s.at[to], r2r.at[to], zdev).wait_send()
        rcopy(es.at[0], er.at[0, 0], rets.at[to], retr.at[to], zdev).wait_send()

    @pl.loop(0, experts)
    def _(k):
        near = ((2 * k) % zr + zr - z) % zr // (zr // 2)

        @pl.when(2 * k + near != me)
        def _():
            for a in range(2):
                rcopy(sx.at[a, 0], rx.at[a, 0], p1s.at[a, k], p1r.at[a, 0], zdev).wait_send()

    @pl.loop(0, ne // 2)
    def _(i):
        source = near_home(i, -zdir)
        for a in range(2):
            ref = rx.at[a, source, 1 - h]
            rcopy(ref, ref, fws.at[a, source], p1r.at[a, source], zdev).wait_send()

    @pl.loop(1, nt)
    def _(d):
        to = (t + d) % nt
        rcopy(rp.at[0], rq.at[0], r1s.at[to], r1r.at[to], zdev).wait_send()
        rcopy(rxs, ry.at[0], r3s.at[to], r3r.at[to], zdev).wait_send()

    @pl.loop(0, groups // 2)
    def _(j):
        rcopy(rb.at[j], cb.at[j], cs.at[j], cr.at[j], zdev).wait_send()

    for copy in pending:
        copy.wait_send()
    for copy in out_copies:
        copy.wait()


def hand_kernel(*refs):
    ins, outs, bufs = refs[:4], refs[4:8], refs[8:12]
    sin, sout = refs[12], refs[13]
    copies = []
    for n, (src, buf, dst) in enumerate(zip(ins, bufs, outs)):
        parts = 4 if src.shape[0] * src.shape[1] >= 1 << 19 else 1
        step = src.shape[0] // parts
        for k in range(parts):
            at = pl.ds(k * step, step)
            there = pltpu.make_async_copy(src.at[at], buf.at[at], sin.at[n, k])
            back = pltpu.make_async_copy(buf.at[at], dst.at[at], sout.at[n, k])
            there.start()
            copies.append((there, back))
    for there, back in copies:
        there.wait()
        back.start()
    for _, back in copies:
        back.wait()


def hand_out(*arrays):
    aspec = pl.BlockSpec(memory_space=pl.ANY)
    return pl.pallas_call(
        hand_kernel,
        out_shape=tuple(jax.ShapeDtypeStruct(v.shape, v.dtype) for v in arrays),
        in_specs=[aspec] * 4,
        out_specs=(aspec,) * 4,
        scratch_shapes=[pltpu.VMEM(v.shape, v.dtype) for v in arrays]
        + [pltpu.SemaphoreType.DMA((4, 4)), pltpu.SemaphoreType.DMA((4, 4))],
        name="hand_out",
    )(*arrays)


def body(tokens, cotangent, w_in, w_out, router, chosen):
    tok_dev, features = tokens.shape
    hidden = w_in.shape[1]
    ne = lax.axis_size("expert")
    nt = lax.axis_size("tensor")
    bucket = 4 * tok_dev // ne
    experts, cap = chosen.shape
    feat = features // nt
    share = feat // 2
    groups = features // share

    vm = lambda shape, kind: pltpu.VMEM(shape, kind)
    dma = lambda *shape: pltpu.SemaphoreType.DMA(shape)
    vspec = pl.BlockSpec(memory_space=pltpu.VMEM)
    aspec = pl.BlockSpec(memory_space=pl.ANY)
    half, quarter = cap // 2, cap // 4
    g2 = groups // 2
    scratch = [
        vm((experts, cap), F32),
        vm((8, features), F32),
        vm((experts * bucket, tok_dev), BF),
        vm((8, cap), F32),
        vm((cap, 128), F32),
        vm((2, tok_dev, feat), BF),
        vm((features, hidden), BF),
        vm((hidden, features), BF),
        vm((2, experts, 2, bucket, share), BF),
        vm((2, ne, 2, bucket, share), BF),
        vm((2, groups, cap, share), BF),
        vm((2, cap, hidden), F32),
        vm((cap, share), F32),
        vm((cap, hidden), BF),
        vm((cap, hidden), BF),
        vm((cap, 128), F32),
        vm((g2, cap, share), BF),
        vm((g2, cap, share), BF),
        vm((RING, half, share), BF),
        vm((2, 2, quarter, share), BF),
        vm((2, 2, half, share), BF),
        vm((2, quarter, share), BF),
        vm((2, half, share), BF),
        vm((half, share), BF),
        vm((8, 128), F32),
        vm((cap, share), BF),
        vm((ne, bucket, share), BF),
        vm((experts, 2, bucket, share), BF),
        vm((features, hidden), BF),
        vm((hidden, features), BF),
        vm((nt, 2, 8, share), F32),
        vm((nt, 2, 8, share), F32),
        vm((2, 8, share), F32),
        vm((8, share), F32),
        vm((8, share), F32),
        vm((ne, 8, share), F32),
        vm((experts, feat), F32),
        vm((nt, experts, feat), F32),
        dma(4), dma(2, experts), dma(2, ne), dma(2, ne), dma(2, 2, 2), dma(2, 2, 2), dma(2, g2, 2, 4), dma(2, groups, 2),
        dma(g2), dma(g2), dma(RING), dma(RING), dma(2, 2), dma(2, 2), dma(2, 2), dma(2, 2),
        dma(2), dma(2), dma(2), dma(2), pltpu.SemaphoreType.DMA, pltpu.SemaphoreType.DMA,
        dma(ne), dma(ne), dma(nt), dma(nt), pltpu.SemaphoreType.DMA, pltpu.SemaphoreType.DMA,
        dma(ne), dma(ne), dma(nt), dma(nt), dma(2),
    ]
    gt, gin, gout, gr = pl.pallas_call(
        functools.partial(step_kernel, ne, nt, bucket),
        out_shape=(
            jax.ShapeDtypeStruct((tok_dev, feat), BF),
            jax.ShapeDtypeStruct((features, hidden), BF),
            jax.ShapeDtypeStruct((hidden, features), BF),
            jax.ShapeDtypeStruct((experts, features), F32),
        ),
        in_specs=[aspec, aspec, aspec, aspec, vspec, vspec],
        out_specs=(vspec, aspec, aspec, vspec),
        scratch_shapes=scratch,
        compiler_params=pltpu.CompilerParams(
            collective_id=0, has_side_effects=True, vmem_limit_bytes=60 * 1024 * 1024
        ),
        name="moe_step",
    )(
        tokens, cotangent, w_in, w_out, router.T, chosen,
    )
    gt, gin, gout, gr = hand_out(gt, gin, gout, gr)
    return gt, gin, gout, gr.T


def solution(mesh):
    placed = (
        P("expert", None),
        P("expert", None),
        P(None, ("expert", "tensor")),
        P(("expert", "tensor"), None),
        P(),
        P(),
    )
    return jax.shard_map(
        body,
        mesh=mesh,
        in_specs=placed,
        out_specs=(
            P("expert", "tensor"),
            P(None, ("expert", "tensor")),
            P(("expert", "tensor"), None),
            P(),
        ),
        check_vma=False,
    )
```

```python
import functools

import jax
import jax.numpy as jnp
from jax import lax
from jax.experimental import pallas as pl
from jax.experimental.pallas import tpu as pltpu
from jax.sharding import PartitionSpec as P

MESH = pl.DeviceIdType.MESH
BF = jnp.bfloat16
F32 = jnp.float32
RING = 4


def mm(a, b, dims):
    return lax.dot_general(a, b, (dims, ((), ())), preferred_element_type=F32)


def step_kernel(
    ne, nt, bucket,
    tok, cot, w_in, w_out, rt_any, chosen_any,
    gt, gin, gout, gr,
    chosen, rt, rrow, hot, q_row, q_col,
    tv, w1v, w2v, sx, rx, gx, acc, gp, hg, da, dsb, rb, cb, zb, yi, yj, yk, yl, zf, fv, fb, es, er,
    ginv, goutv, rp, rq, rs1, rz, rv, rw, rxs, ry,
    ld, p1s, p1r, pcs, pcr, ags, agr, cs, cr, zzs, zzr, yis, yir, yjs, yjr, yks, ykr, yls, ylr, zfs, zfr,
    rets, retr, r1s, r1r, rzs, rzr, r2s, r2r, r3s, r3r, outs,
):
    me = lax.axis_index("expert")
    t = lax.axis_index("tensor")
    h = me % 2
    y = t // 2
    c = t % 2
    feat = tv.shape[2]
    share = feat // 2
    cap = hg.shape[0]
    groups = gx.shape[1]
    half = cap // 2
    quarter = cap // 4

    zdev = (me + 1 - 2 * h, t)
    cdev = (me, 2 * y + 1 - c)
    yn = (y + 1) % RING
    yp = (y + 3) % RING
    yo = (y + 2) % RING
    ynd = (me, 2 * yn + c)
    ypd = (me, 2 * yp + c)

    def rcopy(src, dst, ss, rs, dev):
        return pltpu.make_async_remote_copy(
            src_ref=src, dst_ref=dst, send_sem=ss, recv_sem=rs, device_id=dev, device_id_type=MESH
        )

    pending = []

    def send(src, dst, ss, rs, dev):
        copy = rcopy(src, dst, ss, rs, dev)
        copy.start()
        pending.append(copy)

    def arrived(dst, rs):
        rcopy(dst, dst, rs, rs, zdev).wait_recv()

    loads = [
        pltpu.make_async_copy(tok.at[:, pl.ds(pl.multiple_of(t * feat, feat), feat)], tv.at[0], ld.at[0]),
        pltpu.make_async_copy(cot.at[:, pl.ds(pl.multiple_of(t * feat, feat), feat)], tv.at[1], ld.at[1]),
        pltpu.make_async_copy(w_in, w1v, ld.at[2]),
        pltpu.make_async_copy(w_out, w2v, ld.at[3]),
    ]
    load_chosen = pltpu.make_async_copy(chosen_any, chosen, ld.at[4])
    load_router = pltpu.make_async_copy(rt_any, rt, ld.at[5])
    load_chosen.start()
    loads[0].start()
    loads[1].start()
    load_router.start()
    loads[2].start()
    loads[3].start()

    barrier = pltpu.get_barrier_semaphore()

    @pl.loop(1, ne)
    def _(d):
        pl.semaphore_signal(barrier, inc=1, device_id=((me + d) % ne, t), device_id_type=MESH)

    @pl.loop(1, nt)
    def _(d):
        pl.semaphore_signal(barrier, inc=1, device_id=(me, (t + d) % nt), device_id_type=MESH)

    experts = chosen.shape[0]
    tok_dev = tv.shape[1]
    slots = experts * bucket
    first = (me * tok_dev).astype(F32)
    col = lax.broadcasted_iota(jnp.int32, (bucket, cap), 1).astype(F32)
    row = lax.broadcasted_iota(jnp.int32, (bucket, cap), 0).astype(F32)
    tok_at = lax.broadcasted_iota(jnp.int32, (bucket, tok_dev), 1).astype(F32)
    load_chosen.wait()
    picks = chosen[...].astype(F32)
    starts = jnp.sum(jnp.where(picks < first, 1.0, 0.0), axis=1, keepdims=True)
    ahead = picks + 1.0
    for k in range(experts):
        match = col == row + starts[k:k + 1, :]
        held = jnp.sum(jnp.where(match, ahead[k:k + 1, :], 0.0), axis=1, keepdims=True) - 1.0 - first
        hot[k * bucket:(k + 1) * bucket, :] = jnp.where(tok_at == held, 1.0, 0.0).astype(BF)

    for a in range(2):
        loads[a].wait()
        for k in range(2):
            packed = mm(hot[...], tv[a, :, k * share:(k + 1) * share], ((1,), (0,))).astype(BF)
            sx[a, :, k] = packed.reshape(slots // bucket, bucket, share)
        if a == 0:
            pl.semaphore_wait(barrier, ne + nt - 2)

        @pl.loop(1, ne)
        def _(d):
            to = (me + d) % ne
            rcopy(sx.at[a, to // 2, to % 2], rx.at[a, me], p1s.at[a, to], p1r.at[a, me], (to, t)).start()

        rx[a, me] = sx[a, me // 2, h]

    home_row = lax.broadcasted_iota(jnp.int32, (ne, cap), 0).astype(F32)
    place = lax.broadcasted_iota(jnp.int32, (ne, cap), 1).astype(F32)
    mine_row = jnp.sum(
        jnp.where(lax.broadcasted_iota(jnp.int32, (experts, cap), 0) == me // 2, chosen[...], 0).astype(F32),
        axis=0, keepdims=True,
    )
    low_bound = home_row * float(tok_dev)
    before = jnp.sum(jnp.where(mine_row < low_bound, 1.0, 0.0), axis=1, keepdims=True)
    inside = jnp.logical_and(mine_row >= low_bound, mine_row < low_bound + float(tok_dev))
    q = jnp.sum(jnp.where(inside, home_row * float(bucket) + place - before, 0.0), axis=0, keepdims=True)
    q_row[...] = jnp.broadcast_to(q, q_row.shape)
    q_col[...] = jnp.transpose(jnp.broadcast_to(q, (128, cap)))
    load_router.wait()
    router_all = rt[...].astype(F32)
    rrow[...] = jnp.broadcast_to(
        jnp.sum(
            jnp.where(lax.broadcasted_iota(jnp.int32, router_all.shape, 0) == me // 2, router_all, 0.0),
            axis=0, keepdims=True,
        ),
        rrow.shape,
    )

    own_g = 4 * y + 2 * c + h

    cut = (half + quarter // 2, half)

    def part_rows(a, part):
        return pl.ds(part * cut[a], cut[a] if part == 0 else cap - cut[a])

    def fan(a, y_, h_, target, part=None):
        g = 4 * y_ + 2 * c + h_
        j = 2 * y_ + h_
        dev = (zdev, ynd, ypd, cdev)[target]
        if part is None:
            ref = gx.at[a, g]
            send(ref, ref, ags.at[a, j, 0, target], agr.at[a, g, 0], dev)
        else:
            ref = gx.at[a, g, part_rows(a, part)]
            send(ref, ref, ags.at[a, j, part, target], agr.at[a, g, part], dev)

    def got(a, y_, h_):
        g = 4 * y_ + 2 * c + h_
        arrived(gx.at[a, g], agr.at[a, g, 0])

    def got_halves(a, y_, h_):
        g = 4 * y_ + 2 * c + h_
        for part in range(2):
            arrived(gx.at[a, g, part_rows(a, part)], agr.at[a, g, part])

    Z, N, B, C = 0, 1, 2, 3
    rows = 128

    buckets = ne * bucket
    def dispatched(a):
        @pl.loop(1, ne)
        def _(d):
            source = (me + ne - d) % ne
            arrived(rx.at[a, source], p1r.at[a, source])

    def compact(a):
        @pl.loop(0, cap // rows)
        def _(i):
            at = pl.ds(pl.multiple_of(i * rows, rows), rows)
            slot = lax.broadcasted_iota(jnp.int32, (rows, buckets), 1).astype(F32)
            pick = jnp.where(slot == q_col[at, 0:1], 1.0, 0.0).astype(BF)
            gx[a, own_g, at] = mm(pick, rx[a].reshape(buckets, share), ((1,), (0,))).astype(BF)

    acc[...] = jnp.zeros_like(acc)
    gp[...] = jnp.zeros_like(gp)

    def block_at(g):
        return pl.ds(pl.multiple_of(g * share, share), share)

    def add_x(g):
        x = gx[0, g]
        acc[0] += mm(x, w1v[block_at(g), :], ((1,), (0,)))
        gp[...] += x.astype(F32) * rrow[0:1, block_at(g)]

    def add_y(g):
        acc[1] += mm(gx[1, g], w2v[:, block_at(g)], ((1,), (1,)))

    def use(a, y_):
        @pl.loop(0, 2)
        def _(k):
            g = 4 * y_ + 2 * c + k
            o = 4 * y_ + 2 * (1 - c) + k
            (add_x, add_y)[a](g)
            arrived(gx.at[a, o], agr.at[a, o, 0])
            (add_x, add_y)[a](o)

    def got_half(a, y_, h_, part):
        g = 4 * y_ + 2 * c + h_
        arrived(gx.at[a, g, part_rows(a, part)], agr.at[a, g, part])

    def piece(a, y_, h_, part, k):
        g = 4 * y_ + 2 * c + h_
        whole = part_rows(a, part)
        return gx.at[a, g, pl.ds(whole.start + k * (whole.size // 2), whole.size // 2)]

    def relay(y_, h_, part, k, target):
        ref = piece(0, y_, h_, part, k)
        send(ref, ref, pcs.at[h_, part, k], pcr.at[h_, part, k], (zdev, ynd, ypd, cdev)[target])

    def got_pieces(y_, h_, part):
        for k in range(2):
            arrived(piece(0, y_, h_, part, k), pcr.at[h_, part, k])

    dispatched(0)
    compact(0)
    fan(0, y, h, N, 1)
    fan(0, y, h, B, 1)
    fan(0, y, h, N, 0)
    fan(0, y, h, B, 0)
    fan(0, y, h, Z, 1)
    fan(0, y, h, Z, 0)
    fan(0, y, h, C)
    for part in (1, 0):
        got_half(0, yp, h, part)
        relay(yp, h, part, 0, N)
        got_half(0, yn, h, part)
        relay(yn, h, part, 1, B)
    fan(0, yp, h, C)
    fan(0, yn, h, C)
    dispatched(1)
    compact(1)
    fan(1, y, h, Z)
    fan(1, y, h, N)
    fan(1, y, h, B)
    fan(1, y, h, C)
    fan(0, yp, h, Z, 0)
    fan(0, yn, h, Z, 0)
    got_pieces(yo, h, 0)
    fan(0, yo, h, Z, 0)
    got_pieces(yo, h, 1)
    fan(0, yo, h, C)
    loads[2].wait()
    got_half(0, y, 1 - h, 1)
    fan(0, y, 1 - h, N, 1)
    fan(0, y, 1 - h, B, 1)
    got_half(0, y, 1 - h, 0)
    fan(0, y, 1 - h, C)
    use(0, y)
    got(1, yp, h)
    fan(1, yp, h, N, 0)
    fan(1, yp, h, C)
    got(1, yn, h)
    fan(1, yn, h, B, 1)
    fan(1, yn, h, C)
    got(1, y, 1 - h)
    fan(1, y, 1 - h, N)
    fan(1, y, 1 - h, B)
    fan(1, y, 1 - h, C)
    loads[3].wait()
    got_half(0, yp, 1 - h, 1)
    relay(yp, 1 - h, 1, 0, N)
    got_half(0, yn, 1 - h, 1)
    relay(yn, 1 - h, 1, 1, B)
    use(1, y)
    got_halves(1, yo, h)
    fan(1, yo, h, C)
    got_half(0, yp, 1 - h, 0)
    fan(0, yp, 1 - h, C)
    got_half(0, yn, 1 - h, 0)
    fan(0, yn, 1 - h, C)
    use(0, yp)
    got(1, yp, 1 - h)
    fan(1, yp, 1 - h, N, 0)
    fan(1, yp, 1 - h, C)
    got(1, yn, 1 - h)
    fan(1, yn, 1 - h, B, 1)
    fan(1, yn, 1 - h, C)
    use(0, yn)
    got_half(0, yo, 1 - h, 0)
    got_pieces(yo, 1 - h, 1)
    fan(0, yo, 1 - h, C)
    use(1, yp)
    use(0, yo)
    use(1, yn)
    got_halves(1, yo, 1 - h)
    fan(1, yo, 1 - h, C)
    use(1, yo)

    er_rows = 64

    @pl.loop(0, cap // er_rows)
    def _(i):
        at = pl.ds(pl.multiple_of(i * er_rows, er_rows), er_rows)
        gate = jax.nn.sigmoid(jnp.sum(gp[at, :], axis=1, keepdims=True))
        pre = acc[0, at, :]
        up = acc[1, at, :]
        sig = jax.nn.sigmoid(pre)
        hidden = pre * sig
        hg[at, :] = (gate * hidden).astype(BF)
        gate_grad = jnp.sum(hidden * up, axis=1, keepdims=True)
        da[at, :] = (gate * up * sig * (1.0 + pre * (1.0 - sig))).astype(BF)
        score = gate_grad * gate * (1.0 - gate)
        dsb[at, :] = jnp.broadcast_to(score, (er_rows, dsb.shape[1]))

    def r_value(g):
        s = dsb[...]
        wide = jnp.concatenate([s, s], axis=1)
        return mm(da[...], w1v[block_at(g), :], ((1,), (1,))) + wide * rrow[0:1, block_at(g)]

    low = pl.ds(0, half)
    high = pl.ds(half, half)

    def partner(place_y):
        @pl.loop(0, 2)
        def _(k):
            i = 2 * place_y + k
            rb[i] = r_value(4 * place_y + 2 * (1 - c) + k).astype(BF)
            rcopy(rb.at[i], cb.at[i], cs.at[i], cr.at[i], cdev).start()

    def sums(place_y):
        @pl.loop(0, 2)
        def _(k):
            j = 2 * place_y + k
            value = r_value(4 * place_y + 2 * c + k)
            arrived(cb.at[j], cr.at[j])
            cb[j] = (cb[j].astype(F32) + value).astype(BF)

        send(cb.at[2 * place_y + 1 - h, low], zb.at[place_y], zzs.at[place_y], zzr.at[place_y], zdev)

    partner(yo)
    partner(yp)
    sums(yo)
    for k in range(2):
        send(cb.at[2 * yo + k, pl.ds(half, quarter)], yi.at[k, 0], yis.at[k, 0], yir.at[k, 0], ynd)
        send(cb.at[2 * yo + k, pl.ds(half + quarter, quarter)], yi.at[k, 1], yis.at[k, 1], yir.at[k, 1], ypd)
    partner(yn)
    sums(yp)
    partner(y)
    sums(yn)
    sums(y)

    def add_z(k):
        arrived(zb.at[k], zzr.at[k])
        zb[k] = (zb[k].astype(F32) + cb[2 * k + h, low].astype(F32)).astype(BF)

    add_z(yo)
    send(zb.at[yo, pl.ds(0, quarter)], yk.at[0], yks.at[0], ykr.at[0], ynd)
    send(zb.at[yo, pl.ds(quarter, quarter)], yk.at[1], yks.at[1], ykr.at[1], ypd)
    for k in range(2):
        arrived(yi.at[k, 0], yir.at[k, 0])
        arrived(yi.at[k, 1], yir.at[k, 1])
        first = pl.ds(half, quarter)
        second = pl.ds(half + quarter, quarter)
        cb[2 * yn + k, first] = (cb[2 * yn + k, first].astype(F32) + yi[k, 0].astype(F32)).astype(BF)
        cb[2 * yp + k, second] = (cb[2 * yp + k, second].astype(F32) + yi[k, 1].astype(F32)).astype(BF)
        send(cb.at[2 * yn + k, high], yj.at[k, 0], yjs.at[k, 0], yjr.at[k, 0], ynd)
        send(cb.at[2 * yp + k, high], yj.at[k, 1], yjs.at[k, 1], yjr.at[k, 1], ypd)

    s = dsb[...]
    s_hi = s.astype(BF).astype(F32)
    s_mid = (s - s_hi).astype(BF).astype(F32)
    s_lo = s - s_hi - s_mid
    lane = lax.broadcasted_iota(jnp.int32, s.shape, 1)
    terms = jnp.where(lane == 0, s_hi, jnp.where(lane == 1, s_mid, jnp.where(lane == 2, s_lo, 0.0)))
    terms = jnp.transpose(terms)[:16].astype(BF)

    @pl.loop(0, groups)
    def _(g):
        rp[g // 2, g % 2] = mm(terms, gx[0, g], ((1,), (0,)))[:8]

    @pl.loop(1, nt)
    def _(d):
        to = (t + d) % nt
        rcopy(rp.at[to], rq.at[t], r1s.at[to], r1r.at[t], (me, to)).start()

    def weight_grads(first, count):
        @pl.loop(first, first + count)
        def _(g):
            goutv[:, block_at(g)] = mm(hg[...], gx[1, g], ((0,), (0,))).astype(BF)
            ginv[block_at(g), :] = mm(gx[0, g], da[...], ((0,), (0,))).astype(BF)

    @pl.loop(1, nt)
    def _(d):
        source = (t + nt - d) % nt
        arrived(rq.at[source], r1r.at[source])

    rq[t] = rp[t]
    total = rq[0]
    for k in range(1, nt):
        total = total + rq[k]
    rs1[...] = total
    send(rs1.at[1 - h], rz, rzs, rzr, zdev)

    weight_grads(0, 4)
    add_z(yp)
    add_z(yn)
    first = pl.ds(0, quarter)
    second = pl.ds(quarter, quarter)
    for k in range(2):
        arrived(yk.at[k], ykr.at[k])
    zb[yn, first] = (zb[yn, first].astype(F32) + yk[0].astype(F32)).astype(BF)
    zb[yp, second] = (zb[yp, second].astype(F32) + yk[1].astype(F32)).astype(BF)
    send(zb.at[yn], yl.at[0], yls.at[0], ylr.at[0], ynd)
    send(zb.at[yp], yl.at[1], yls.at[1], ylr.at[1], ypd)
    base = 2 * y + 1 - h
    for k in range(2):
        for n in range(2):
            arrived(yj.at[k, n], yjr.at[k, n])
    cb[base, high] = (
        cb[base, high].astype(F32) + (yj[1 - h, 0].astype(F32) + yj[1 - h, 1].astype(F32))
    ).astype(BF)
    send(cb.at[base, high], zf, zfs, zfr, zdev)

    weight_grads(4, 6)

    mine = 2 * y + h
    arrived(zb.at[y], zzr.at[y])
    arrived(zf, zfr)
    fb[high, :] = (
        cb[mine, high].astype(F32) + (yj[h, 0].astype(F32) + yj[h, 1].astype(F32)) + zf[...].astype(F32)
    ).astype(BF)
    for side in range(2):
        arrived(yl.at[side], ylr.at[side])
    fb[low, :] = (
        cb[mine, low].astype(F32) + zb[y].astype(F32) + (yl[0].astype(F32) + yl[1].astype(F32))
    ).astype(BF)

    arrived(rz, rzr)
    router_sum = jnp.sum(rs1[h] + rz[...], axis=0, keepdims=True)
    rv[...] = jnp.broadcast_to(router_sum, rv.shape)
    rw[me] = jnp.broadcast_to(router_sum, rv.shape)

    @pl.loop(1, ne)
    def _(d):
        to = (me + d) % ne
        rcopy(rv, rw.at[me], r2s.at[to], r2r.at[me], (to, t)).start()

    homes = rows // bucket

    @pl.loop(0, ne // homes)
    def _(i):
        chunk = (i + me // homes) % (ne // homes)
        spread = (
            (lax.broadcasted_iota(jnp.int32, (rows, cap), 0) + chunk * rows).astype(F32) == q_row[0:1, :]
        ).astype(BF)
        es[pl.ds(chunk * homes, homes)] = (
            mm(spread, fb[...], ((1,), (0,))).astype(BF).reshape(homes, bucket, share)
        )

        @pl.loop(0, homes)
        def _(k):
            to = chunk * homes + (me + k) % homes

            @pl.when(to != me)
            def _():
                rcopy(es.at[to], er.at[me // 2, h], rets.at[to], retr.at[me], (to, t)).start()

    er[me // 2, h] = es[me]

    weight_grads(10, 6)
    out_copies = [
        pltpu.make_async_copy(ginv, gin, outs.at[0]),
        pltpu.make_async_copy(goutv, gout, outs.at[1]),
    ]
    for copy in out_copies:
        copy.start()

    @pl.loop(1, ne)
    def _(d):
        source = (me + ne - d) % ne
        arrived(rw.at[source], r2r.at[source])

    for k in range(ne):
        rxs[k // 2:k // 2 + 1, (k % 2) * share:(k % 2 + 1) * share] = rw[k, 0:1, :]
    ry[t] = rxs[...]

    @pl.loop(1, nt)
    def _(d):
        to = (t + d) % nt
        rcopy(rxs, ry.at[t], r3s.at[to], r3r.at[t], (me, to)).start()

    @pl.loop(1, nt)
    def _(d):
        source = (t + nt - d) % nt
        arrived(ry.at[source], r3r.at[source])

    for k in range(nt):
        gr[:, k * feat:(k + 1) * feat] = ry[k]

    @pl.loop(1, ne)
    def _(d):
        source = (me + ne - d) % ne
        arrived(er.at[source // 2, source % 2], retr.at[source])

    for k in range(2):
        gt[:, k * share:(k + 1) * share] = mm(hot[...], er[:, k].reshape(slots, share), ((0,), (0,))).astype(BF)

    @pl.loop(1, ne)
    def _(d):
        to = (me + d) % ne
        for a in range(2):
            rcopy(sx.at[a, 0, 0], rx.at[a, 0], p1s.at[a, to], p1r.at[a, to], zdev).wait_send()
        rcopy(rv, rw.at[0], r2s.at[to], r2r.at[to], zdev).wait_send()
        rcopy(es.at[0], er.at[0, 0], rets.at[to], retr.at[to], zdev).wait_send()

    @pl.loop(1, nt)
    def _(d):
        to = (t + d) % nt
        rcopy(rp.at[0], rq.at[0], r1s.at[to], r1r.at[to], zdev).wait_send()
        rcopy(rxs, ry.at[0], r3s.at[to], r3r.at[to], zdev).wait_send()

    @pl.loop(0, groups // 2)
    def _(j):
        rcopy(rb.at[j], cb.at[j], cs.at[j], cr.at[j], zdev).wait_send()

    for copy in pending:
        copy.wait_send()
    for copy in out_copies:
        copy.wait()


def hand_kernel(*refs):
    ins, outs, bufs = refs[:4], refs[4:8], refs[8:12]
    sin, sout = refs[12], refs[13]
    copies = []
    for n, (src, buf, dst) in enumerate(zip(ins, bufs, outs)):
        parts = 4 if src.shape[0] * src.shape[1] >= 1 << 19 else 1
        step = src.shape[0] // parts
        for k in range(parts):
            at = pl.ds(k * step, step)
            there = pltpu.make_async_copy(src.at[at], buf.at[at], sin.at[n, k])
            back = pltpu.make_async_copy(buf.at[at], dst.at[at], sout.at[n, k])
            there.start()
            copies.append((there, back))
    for there, back in copies:
        there.wait()
        back.start()
    for _, back in copies:
        back.wait()


def hand_out(*arrays):
    aspec = pl.BlockSpec(memory_space=pl.ANY)
    return pl.pallas_call(
        hand_kernel,
        out_shape=tuple(jax.ShapeDtypeStruct(v.shape, v.dtype) for v in arrays),
        in_specs=[aspec] * 4,
        out_specs=(aspec,) * 4,
        scratch_shapes=[pltpu.VMEM(v.shape, v.dtype) for v in arrays]
        + [pltpu.SemaphoreType.DMA((4, 4)), pltpu.SemaphoreType.DMA((4, 4))],
        name="hand_out",
    )(*arrays)


def body(tokens, cotangent, w_in, w_out, router, chosen):
    tok_dev, features = tokens.shape
    hidden = w_in.shape[1]
    ne = lax.axis_size("expert")
    nt = lax.axis_size("tensor")
    bucket = 4 * tok_dev // ne
    experts, cap = chosen.shape
    feat = features // nt
    share = feat // 2
    groups = features // share

    vm = lambda shape, kind: pltpu.VMEM(shape, kind)
    dma = lambda *shape: pltpu.SemaphoreType.DMA(shape)
    vspec = pl.BlockSpec(memory_space=pltpu.VMEM)
    aspec = pl.BlockSpec(memory_space=pl.ANY)
    half, quarter = cap // 2, cap // 4
    g2 = groups // 2
    scratch = [
        vm((experts, cap), jnp.int32),
        vm((experts, features), BF),
        vm((8, features), F32),
        vm((experts * bucket, tok_dev), BF),
        vm((8, cap), F32),
        vm((cap, 128), F32),
        vm((2, tok_dev, feat), BF),
        vm((features, hidden), BF),
        vm((hidden, features), BF),
        vm((2, experts, 2, bucket, share), BF),
        vm((2, ne, bucket, share), BF),
        vm((2, groups, cap, share), BF),
        vm((2, cap, hidden), F32),
        vm((cap, share), F32),
        vm((cap, hidden), BF),
        vm((cap, hidden), BF),
        vm((cap, 128), F32),
        vm((g2, cap, share), BF),
        vm((g2, cap, share), BF),
        vm((RING, half, share), BF),
        vm((2, 2, quarter, share), BF),
        vm((2, 2, half, share), BF),
        vm((2, quarter, share), BF),
        vm((2, half, share), BF),
        vm((half, share), BF),
        vm((8, 128), F32),
        vm((cap, share), BF),
        vm((ne, bucket, share), BF),
        vm((experts, 2, bucket, share), BF),
        vm((features, hidden), BF),
        vm((hidden, features), BF),
        vm((nt, 2, 8, share), F32),
        vm((nt, 2, 8, share), F32),
        vm((2, 8, share), F32),
        vm((8, share), F32),
        vm((8, share), F32),
        vm((ne, 8, share), F32),
        vm((experts, feat), F32),
        vm((nt, experts, feat), F32),
        dma(6), dma(2, ne), dma(2, ne), dma(2, 2, 2), dma(2, 2, 2), dma(2, g2, 2, 4), dma(2, groups, 2),
        dma(g2), dma(g2), dma(RING), dma(RING), dma(2, 2), dma(2, 2), dma(2, 2), dma(2, 2),
        dma(2), dma(2), dma(2), dma(2), pltpu.SemaphoreType.DMA, pltpu.SemaphoreType.DMA,
        dma(ne), dma(ne), dma(nt), dma(nt), pltpu.SemaphoreType.DMA, pltpu.SemaphoreType.DMA,
        dma(ne), dma(ne), dma(nt), dma(nt), dma(2),
    ]
    gt, gin, gout, gr = pl.pallas_call(
        functools.partial(step_kernel, ne, nt, bucket),
        out_shape=(
            jax.ShapeDtypeStruct((tok_dev, feat), BF),
            jax.ShapeDtypeStruct((features, hidden), BF),
            jax.ShapeDtypeStruct((hidden, features), BF),
            jax.ShapeDtypeStruct((experts, features), F32),
        ),
        in_specs=[aspec] * 6,
        out_specs=(vspec, aspec, aspec, vspec),
        scratch_shapes=scratch,
        compiler_params=pltpu.CompilerParams(
            collective_id=0, has_side_effects=True, vmem_limit_bytes=60 * 1024 * 1024
        ),
        name="moe_step",
    )(
        tokens, cotangent, w_in, w_out, router.T, chosen,
    )
    gt, gin, gout, gr = hand_out(gt, gin, gout, gr)
    return gt, gin, gout, gr.T


def solution(mesh):
    placed = (
        P("expert", None),
        P("expert", None),
        P(None, ("expert", "tensor")),
        P(("expert", "tensor"), None),
        P(),
        P(),
    )
    return jax.shard_map(
        body,
        mesh=mesh,
        in_specs=placed,
        out_specs=(
            P("expert", "tensor"),
            P(None, ("expert", "tensor")),
            P(("expert", "tensor"), None),
            P(),
        ),
        check_vma=False,
    )
```

```python
import functools

import jax
import jax.numpy as jnp
from jax import lax
from jax.experimental import pallas as pl
from jax.experimental.pallas import tpu as pltpu
from jax.sharding import PartitionSpec as P

MESH = pl.DeviceIdType.MESH
BF = jnp.bfloat16
F32 = jnp.float32
RING = 4


def mm(a, b, dims):
    return lax.dot_general(a, b, (dims, ((), ())), preferred_element_type=F32)


def step_kernel(
    ne, nt, bucket,
    tok, cot, w_in, w_out, rt_any, chosen_any,
    gt, gin, gout, gr,
    chosen, rt, rrow, hot, hot_t, gather, spread, q_col,
    tv, w1v, w2v, sx, rx, gx, acc, gp, hg, da, dsb, rb, cb, zb, yi, yj, yk, yl, zf, fv, fb, es, er,
    rp, rq, rs1, rz, rv, rw, rxs, ry,
    ld, p1s, p1r, pcs, pcr, ags, agr, cs, cr, zzs, zzr, yis, yir, yjs, yjr, yks, ykr, yls, ylr, zfs, zfr,
    rets, retr, r1s, r1r, rzs, rzr, r2s, r2r, r3s, r3r,
):
    me = lax.axis_index("expert")
    t = lax.axis_index("tensor")
    h = me % 2
    y = t // 2
    c = t % 2
    feat = tv.shape[2]
    share = feat // 2
    cap = hg.shape[0]
    groups = gx.shape[1]
    half = cap // 2
    quarter = cap // 4

    zdev = (me + 1 - 2 * h, t)
    cdev = (me, 2 * y + 1 - c)
    yn = (y + 1) % RING
    yp = (y + 3) % RING
    yo = (y + 2) % RING
    ynd = (me, 2 * yn + c)
    ypd = (me, 2 * yp + c)

    def rcopy(src, dst, ss, rs, dev):
        return pltpu.make_async_remote_copy(
            src_ref=src, dst_ref=dst, send_sem=ss, recv_sem=rs, device_id=dev, device_id_type=MESH
        )

    pending = []

    def send(src, dst, ss, rs, dev):
        copy = rcopy(src, dst, ss, rs, dev)
        copy.start()
        pending.append(copy)

    def arrived(dst, rs):
        rcopy(dst, dst, rs, rs, zdev).wait_recv()

    loads = [
        pltpu.make_async_copy(tok.at[:, pl.ds(pl.multiple_of(t * feat, feat), feat)], tv.at[0], ld.at[0]),
        pltpu.make_async_copy(cot.at[:, pl.ds(pl.multiple_of(t * feat, feat), feat)], tv.at[1], ld.at[1]),
        pltpu.make_async_copy(w_in, w1v, ld.at[2]),
        pltpu.make_async_copy(w_out, w2v, ld.at[3]),
    ]
    load_chosen = pltpu.make_async_copy(chosen_any, chosen, ld.at[4])
    load_router = pltpu.make_async_copy(rt_any, rt, ld.at[5])
    load_chosen.start()
    loads[0].start()
    loads[1].start()
    load_router.start()
    loads[2].start()
    loads[3].start()

    barrier = pltpu.get_barrier_semaphore()

    @pl.loop(1, ne)
    def _(d):
        pl.semaphore_signal(barrier, inc=1, device_id=((me + d) % ne, t), device_id_type=MESH)

    @pl.loop(1, nt)
    def _(d):
        pl.semaphore_signal(barrier, inc=1, device_id=(me, (t + d) % nt), device_id_type=MESH)

    experts = chosen.shape[0]
    tok_dev = tv.shape[1]
    slots = experts * bucket
    first = (me * tok_dev).astype(F32)
    col = lax.broadcasted_iota(jnp.int32, (bucket, cap), 1).astype(F32)
    row = lax.broadcasted_iota(jnp.int32, (bucket, cap), 0).astype(F32)
    tok_at = lax.broadcasted_iota(jnp.int32, (bucket, tok_dev), 1).astype(F32)
    load_chosen.wait()
    picks = chosen[...].astype(F32)
    starts = jnp.sum(jnp.where(picks < first, 1.0, 0.0), axis=1, keepdims=True)
    ahead = picks + 1.0
    for k in range(experts):
        match = col == row + starts[k:k + 1, :]
        held = jnp.sum(jnp.where(match, ahead[k:k + 1, :], 0.0), axis=1, keepdims=True) - 1.0 - first
        hot[k * bucket:(k + 1) * bucket, :] = jnp.where(tok_at == held, 1.0, 0.0).astype(BF)

    for a in range(2):
        loads[a].wait()
        for k in range(2):
            packed = mm(hot[...], tv[a, :, k * share:(k + 1) * share], ((1,), (0,))).astype(BF)
            sx[a, :, k] = packed.reshape(slots // bucket, bucket, share)
        if a == 0:
            pl.semaphore_wait(barrier, ne + nt - 2)

        @pl.loop(1, ne)
        def _(d):
            to = (me + d) % ne
            rcopy(sx.at[a, to // 2, to % 2], rx.at[a, me], p1s.at[a, to], p1r.at[a, me], (to, t)).start()

        rx[a, me] = sx[a, me // 2, h]

    home_row = lax.broadcasted_iota(jnp.int32, (ne, cap), 0).astype(F32)
    place = lax.broadcasted_iota(jnp.int32, (ne, cap), 1).astype(F32)
    mine_row = jnp.sum(
        jnp.where(lax.broadcasted_iota(jnp.int32, (experts, cap), 0) == me // 2, chosen[...], 0).astype(F32),
        axis=0, keepdims=True,
    )
    low_bound = home_row * float(tok_dev)
    before = jnp.sum(jnp.where(mine_row < low_bound, 1.0, 0.0), axis=1, keepdims=True)
    inside = jnp.logical_and(mine_row >= low_bound, mine_row < low_bound + float(tok_dev))
    q = jnp.sum(jnp.where(inside, home_row * float(bucket) + place - before, 0.0), axis=0, keepdims=True)
    q_col[...] = jnp.transpose(jnp.broadcast_to(q, (128, cap)))
    load_router.wait()
    router_all = rt[...].astype(F32)
    rrow[...] = jnp.broadcast_to(
        jnp.sum(
            jnp.where(lax.broadcasted_iota(jnp.int32, router_all.shape, 0) == me // 2, router_all, 0.0),
            axis=0, keepdims=True,
        ),
        rrow.shape,
    )

    hot_t[...] = jnp.transpose(hot[...].astype(F32)).astype(BF)
    rows = 128

    @pl.loop(0, cap // rows)
    def _(i):
        at = pl.ds(pl.multiple_of(i * rows, rows), rows)
        slot = lax.broadcasted_iota(jnp.int32, (rows, ne * bucket), 1).astype(F32)
        gather[at, :] = jnp.where(slot == q_col[at, 0:1], 1.0, 0.0).astype(BF)

    @pl.loop(0, ne * bucket // rows)
    def _(i):
        at = pl.ds(pl.multiple_of(i * rows, rows), rows)
        slot = (lax.broadcasted_iota(jnp.int32, (rows, cap), 0) + i * rows).astype(F32)
        spread[at, :] = jnp.where(slot == q, 1.0, 0.0).astype(BF)

    own_g = 4 * y + 2 * c + h

    cut = (half + quarter // 2, half)

    def part_rows(a, part):
        return pl.ds(part * cut[a], cut[a] if part == 0 else cap - cut[a])

    def fan(a, y_, h_, target, part=None):
        g = 4 * y_ + 2 * c + h_
        j = 2 * y_ + h_
        dev = (zdev, ynd, ypd, cdev)[target]
        if part is None:
            ref = gx.at[a, g]
            send(ref, ref, ags.at[a, j, 0, target], agr.at[a, g, 0], dev)
        else:
            ref = gx.at[a, g, part_rows(a, part)]
            send(ref, ref, ags.at[a, j, part, target], agr.at[a, g, part], dev)

    def got(a, y_, h_):
        g = 4 * y_ + 2 * c + h_
        arrived(gx.at[a, g], agr.at[a, g, 0])

    def got_halves(a, y_, h_):
        g = 4 * y_ + 2 * c + h_
        for part in range(2):
            arrived(gx.at[a, g, part_rows(a, part)], agr.at[a, g, part])

    Z, N, B, C = 0, 1, 2, 3

    buckets = ne * bucket
    def dispatched(a):
        @pl.loop(1, ne)
        def _(d):
            source = (me + ne - d) % ne
            arrived(rx.at[a, source], p1r.at[a, source])

    def compact(a):
        @pl.loop(0, cap // rows)
        def _(i):
            at = pl.ds(pl.multiple_of(i * rows, rows), rows)
            gx[a, own_g, at] = mm(gather[at, :], rx[a].reshape(buckets, share), ((1,), (0,))).astype(BF)

    acc[...] = jnp.zeros_like(acc)
    gp[...] = jnp.zeros_like(gp)

    def block_at(g):
        return pl.ds(pl.multiple_of(g * share, share), share)

    def add_x(g):
        x = gx[0, g]
        acc[0] += mm(x, w1v[block_at(g), :], ((1,), (0,)))
        gp[...] += x.astype(F32) * rrow[0:1, block_at(g)]

    def add_y(g):
        acc[1] += mm(gx[1, g], w2v[:, block_at(g)], ((1,), (1,)))

    def use(a, y_):
        @pl.loop(0, 2)
        def _(k):
            g = 4 * y_ + 2 * c + k
            o = 4 * y_ + 2 * (1 - c) + k
            (add_x, add_y)[a](g)
            arrived(gx.at[a, o], agr.at[a, o, 0])
            (add_x, add_y)[a](o)

    def got_half(a, y_, h_, part):
        g = 4 * y_ + 2 * c + h_
        arrived(gx.at[a, g, part_rows(a, part)], agr.at[a, g, part])

    def piece(a, y_, h_, part, k):
        g = 4 * y_ + 2 * c + h_
        whole = part_rows(a, part)
        return gx.at[a, g, pl.ds(whole.start + k * (whole.size // 2), whole.size // 2)]

    def relay(y_, h_, part, k, target):
        ref = piece(0, y_, h_, part, k)
        send(ref, ref, pcs.at[h_, part, k], pcr.at[h_, part, k], (zdev, ynd, ypd, cdev)[target])

    def got_pieces(y_, h_, part):
        for k in range(2):
            arrived(piece(0, y_, h_, part, k), pcr.at[h_, part, k])

    dispatched(0)
    compact(0)
    fan(0, y, h, N, 1)
    fan(0, y, h, B, 1)
    fan(0, y, h, N, 0)
    fan(0, y, h, B, 0)
    fan(0, y, h, Z, 1)
    fan(0, y, h, Z, 0)
    fan(0, y, h, C)
    for part in (1, 0):
        got_half(0, yp, h, part)
        relay(yp, h, part, 0, N)
        got_half(0, yn, h, part)
        relay(yn, h, part, 1, B)
    fan(0, yp, h, C)
    fan(0, yn, h, C)
    dispatched(1)
    compact(1)
    fan(1, y, h, Z)
    fan(1, y, h, N)
    fan(1, y, h, B)
    fan(1, y, h, C)
    fan(0, yp, h, Z, 0)
    fan(0, yn, h, Z, 0)
    got_pieces(yo, h, 0)
    fan(0, yo, h, Z, 0)
    got_pieces(yo, h, 1)
    fan(0, yo, h, C)
    loads[2].wait()
    got_half(0, y, 1 - h, 1)
    fan(0, y, 1 - h, N, 1)
    fan(0, y, 1 - h, B, 1)
    got_half(0, y, 1 - h, 0)
    fan(0, y, 1 - h, C)
    use(0, y)
    got(1, yp, h)
    fan(1, yp, h, N, 0)
    fan(1, yp, h, C)
    got(1, yn, h)
    fan(1, yn, h, B, 1)
    fan(1, yn, h, C)
    got(1, y, 1 - h)
    fan(1, y, 1 - h, N)
    fan(1, y, 1 - h, B)
    fan(1, y, 1 - h, C)
    loads[3].wait()
    got_half(0, yp, 1 - h, 1)
    relay(yp, 1 - h, 1, 0, N)
    got_half(0, yn, 1 - h, 1)
    relay(yn, 1 - h, 1, 1, B)
    use(1, y)
    got_halves(1, yo, h)
    fan(1, yo, h, C)
    got_half(0, yp, 1 - h, 0)
    fan(0, yp, 1 - h, C)
    got_half(0, yn, 1 - h, 0)
    fan(0, yn, 1 - h, C)
    use(0, yp)
    got(1, yp, 1 - h)
    fan(1, yp, 1 - h, N, 0)
    fan(1, yp, 1 - h, C)
    got(1, yn, 1 - h)
    fan(1, yn, 1 - h, B, 1)
    fan(1, yn, 1 - h, C)
    use(0, yn)
    got_half(0, yo, 1 - h, 0)
    got_pieces(yo, 1 - h, 1)
    fan(0, yo, 1 - h, C)
    use(1, yp)
    use(0, yo)
    use(1, yn)
    got_halves(1, yo, 1 - h)
    fan(1, yo, 1 - h, C)
    use(1, yo)

    er_rows = 64

    @pl.loop(0, cap // er_rows)
    def _(i):
        at = pl.ds(pl.multiple_of(i * er_rows, er_rows), er_rows)
        gate = jax.nn.sigmoid(jnp.sum(gp[at, :], axis=1, keepdims=True))
        pre = acc[0, at, :]
        up = acc[1, at, :]
        sig = jax.nn.sigmoid(pre)
        hidden = pre * sig
        hg[at, :] = (gate * hidden).astype(BF)
        gate_grad = jnp.sum(hidden * up, axis=1, keepdims=True)
        da[at, :] = (gate * up * sig * (1.0 + pre * (1.0 - sig))).astype(BF)
        score = gate_grad * gate * (1.0 - gate)
        dsb[at, :] = jnp.broadcast_to(score, (er_rows, dsb.shape[1]))

    def r_value(g):
        s = dsb[...]
        wide = jnp.concatenate([s, s], axis=1)
        return mm(da[...], w1v[block_at(g), :], ((1,), (1,))) + wide * rrow[0:1, block_at(g)]

    low = pl.ds(0, half)
    high = pl.ds(half, half)

    def partner(place_y):
        @pl.loop(0, 2)
        def _(k):
            i = 2 * place_y + k
            rb[i] = r_value(4 * place_y + 2 * (1 - c) + k).astype(BF)
            rcopy(rb.at[i], cb.at[i], cs.at[i], cr.at[i], cdev).start()

    def sums(place_y):
        @pl.loop(0, 2)
        def _(k):
            j = 2 * place_y + k
            value = r_value(4 * place_y + 2 * c + k)
            arrived(cb.at[j], cr.at[j])
            cb[j] = (cb[j].astype(F32) + value).astype(BF)

        send(cb.at[2 * place_y + 1 - h, low], zb.at[place_y], zzs.at[place_y], zzr.at[place_y], zdev)

    partner(yo)
    partner(yp)
    sums(yo)
    for k in range(2):
        send(cb.at[2 * yo + k, pl.ds(half, quarter)], yi.at[k, 0], yis.at[k, 0], yir.at[k, 0], ynd)
        send(cb.at[2 * yo + k, pl.ds(half + quarter, quarter)], yi.at[k, 1], yis.at[k, 1], yir.at[k, 1], ypd)
    partner(yn)
    sums(yp)
    partner(y)
    sums(yn)
    sums(y)

    def add_z(k):
        arrived(zb.at[k], zzr.at[k])
        zb[k] = (zb[k].astype(F32) + cb[2 * k + h, low].astype(F32)).astype(BF)

    add_z(yo)
    send(zb.at[yo, pl.ds(0, quarter)], yk.at[0], yks.at[0], ykr.at[0], ynd)
    send(zb.at[yo, pl.ds(quarter, quarter)], yk.at[1], yks.at[1], ykr.at[1], ypd)
    for k in range(2):
        arrived(yi.at[k, 0], yir.at[k, 0])
        arrived(yi.at[k, 1], yir.at[k, 1])
        first = pl.ds(half, quarter)
        second = pl.ds(half + quarter, quarter)
        cb[2 * yn + k, first] = (cb[2 * yn + k, first].astype(F32) + yi[k, 0].astype(F32)).astype(BF)
        cb[2 * yp + k, second] = (cb[2 * yp + k, second].astype(F32) + yi[k, 1].astype(F32)).astype(BF)
        send(cb.at[2 * yn + k, high], yj.at[k, 0], yjs.at[k, 0], yjr.at[k, 0], ynd)
        send(cb.at[2 * yp + k, high], yj.at[k, 1], yjs.at[k, 1], yjr.at[k, 1], ypd)

    s = dsb[...]
    s_hi = s.astype(BF).astype(F32)
    s_mid = (s - s_hi).astype(BF).astype(F32)
    s_lo = s - s_hi - s_mid
    lane = lax.broadcasted_iota(jnp.int32, s.shape, 1)
    terms = jnp.where(lane == 0, s_hi, jnp.where(lane == 1, s_mid, jnp.where(lane == 2, s_lo, 0.0)))
    terms = jnp.transpose(terms)[:16].astype(BF)

    @pl.loop(0, groups)
    def _(g):
        rp[g // 2, g % 2] = mm(terms, gx[0, g], ((1,), (0,)))[:8]

    @pl.loop(1, nt)
    def _(d):
        to = (t + d) % nt
        rcopy(rp.at[to], rq.at[t], r1s.at[to], r1r.at[t], (me, to)).start()

    def weight_grads(first, count):
        @pl.loop(first, first + count)
        def _(g):
            gout[:, block_at(g)] = mm(hg[...], gx[1, g], ((0,), (0,))).astype(BF)
            gin[block_at(g), :] = mm(gx[0, g], da[...], ((0,), (0,))).astype(BF)

    @pl.loop(1, nt)
    def _(d):
        source = (t + nt - d) % nt
        arrived(rq.at[source], r1r.at[source])

    rq[t] = rp[t]
    total = rq[0]
    for k in range(1, nt):
        total = total + rq[k]
    rs1[...] = total
    send(rs1.at[1 - h], rz, rzs, rzr, zdev)

    weight_grads(0, 4)
    add_z(yp)
    add_z(yn)
    first = pl.ds(0, quarter)
    second = pl.ds(quarter, quarter)
    for k in range(2):
        arrived(yk.at[k], ykr.at[k])
    zb[yn, first] = (zb[yn, first].astype(F32) + yk[0].astype(F32)).astype(BF)
    zb[yp, second] = (zb[yp, second].astype(F32) + yk[1].astype(F32)).astype(BF)
    send(zb.at[yn], yl.at[0], yls.at[0], ylr.at[0], ynd)
    send(zb.at[yp], yl.at[1], yls.at[1], ylr.at[1], ypd)
    base = 2 * y + 1 - h
    for k in range(2):
        for n in range(2):
            arrived(yj.at[k, n], yjr.at[k, n])
    cb[base, high] = (
        cb[base, high].astype(F32) + (yj[1 - h, 0].astype(F32) + yj[1 - h, 1].astype(F32))
    ).astype(BF)
    send(cb.at[base, high], zf, zfs, zfr, zdev)

    weight_grads(4, 6)

    mine = 2 * y + h
    arrived(zb.at[y], zzr.at[y])
    arrived(zf, zfr)
    fb[high, :] = (
        cb[mine, high].astype(F32) + (yj[h, 0].astype(F32) + yj[h, 1].astype(F32)) + zf[...].astype(F32)
    ).astype(BF)
    for side in range(2):
        arrived(yl.at[side], ylr.at[side])
    fb[low, :] = (
        cb[mine, low].astype(F32) + zb[y].astype(F32) + (yl[0].astype(F32) + yl[1].astype(F32))
    ).astype(BF)

    arrived(rz, rzr)
    router_sum = jnp.sum(rs1[h] + rz[...], axis=0, keepdims=True)
    rv[...] = jnp.broadcast_to(router_sum, rv.shape)
    rw[me] = jnp.broadcast_to(router_sum, rv.shape)

    @pl.loop(1, ne)
    def _(d):
        to = (me + d) % ne
        rcopy(rv, rw.at[me], r2s.at[to], r2r.at[me], (to, t)).start()

    homes = rows // bucket

    @pl.loop(0, ne // homes)
    def _(i):
        chunk = (i + me // homes) % (ne // homes)
        at = pl.ds(pl.multiple_of(chunk * rows, rows), rows)
        es[pl.ds(chunk * homes, homes)] = (
            mm(spread[at, :], fb[...], ((1,), (0,))).astype(BF).reshape(homes, bucket, share)
        )

        @pl.loop(0, homes)
        def _(k):
            to = chunk * homes + (me + k) % homes

            @pl.when(to != me)
            def _():
                rcopy(es.at[to], er.at[me // 2, h], rets.at[to], retr.at[me], (to, t)).start()

    er[me // 2, h] = es[me]

    weight_grads(10, 6)
    @pl.loop(1, ne)
    def _(d):
        source = (me + ne - d) % ne
        arrived(rw.at[source], r2r.at[source])

    for k in range(ne):
        rxs[k // 2:k // 2 + 1, (k % 2) * share:(k % 2 + 1) * share] = rw[k, 0:1, :]
    ry[t] = rxs[...]

    @pl.loop(1, nt)
    def _(d):
        to = (t + d) % nt
        rcopy(rxs, ry.at[t], r3s.at[to], r3r.at[t], (me, to)).start()

    @pl.loop(1, nt)
    def _(d):
        source = (t + nt - d) % nt
        arrived(ry.at[source], r3r.at[source])

    for k in range(nt):
        gr[:, k * feat:(k + 1) * feat] = ry[k]

    @pl.loop(1, ne)
    def _(d):
        source = (me + ne - d) % ne
        arrived(er.at[source // 2, source % 2], retr.at[source])

    for k in range(2):
        gt[:, k * share:(k + 1) * share] = mm(hot_t[...], er[:, k].reshape(slots, share), ((1,), (0,))).astype(BF)

    @pl.loop(1, ne)
    def _(d):
        to = (me + d) % ne
        for a in range(2):
            rcopy(sx.at[a, 0, 0], rx.at[a, 0], p1s.at[a, to], p1r.at[a, to], zdev).wait_send()
        rcopy(rv, rw.at[0], r2s.at[to], r2r.at[to], zdev).wait_send()
        rcopy(es.at[0], er.at[0, 0], rets.at[to], retr.at[to], zdev).wait_send()

    @pl.loop(1, nt)
    def _(d):
        to = (t + d) % nt
        rcopy(rp.at[0], rq.at[0], r1s.at[to], r1r.at[to], zdev).wait_send()
        rcopy(rxs, ry.at[0], r3s.at[to], r3r.at[to], zdev).wait_send()

    @pl.loop(0, groups // 2)
    def _(j):
        rcopy(rb.at[j], cb.at[j], cs.at[j], cr.at[j], zdev).wait_send()

    for copy in pending:
        copy.wait_send()


def hand_kernel(*refs):
    ins, outs = refs[:4], refs[4:8]
    copies = [pltpu.make_async_copy(a, b, refs[8].at[n]) for n, (a, b) in enumerate(zip(ins, outs))]
    for copy in copies:
        copy.start()
    for copy in copies:
        copy.wait()


def hand_out(*arrays):
    aspec = pl.BlockSpec(memory_space=pl.ANY)
    vspec = pl.BlockSpec(memory_space=pltpu.VMEM)
    return pl.pallas_call(
        hand_kernel,
        out_shape=tuple(jax.ShapeDtypeStruct(v.shape, v.dtype) for v in arrays),
        in_specs=[vspec] * 4,
        out_specs=(aspec,) * 4,
        scratch_shapes=[pltpu.SemaphoreType.DMA((4,))],
        compiler_params=pltpu.CompilerParams(vmem_limit_bytes=16 * 1024 * 1024),
        name="hand_out",
    )(*arrays)


def body(tokens, cotangent, w_in, w_out, router, chosen):
    tok_dev, features = tokens.shape
    hidden = w_in.shape[1]
    ne = lax.axis_size("expert")
    nt = lax.axis_size("tensor")
    bucket = 4 * tok_dev // ne
    experts, cap = chosen.shape
    feat = features // nt
    share = feat // 2
    groups = features // share

    vm = lambda shape, kind: pltpu.VMEM(shape, kind)
    dma = lambda *shape: pltpu.SemaphoreType.DMA(shape)
    vspec = pl.BlockSpec(memory_space=pltpu.VMEM)
    aspec = pl.BlockSpec(memory_space=pl.ANY)
    half, quarter = cap // 2, cap // 4
    g2 = groups // 2
    scratch = [
        vm((experts, cap), jnp.int32),
        vm((experts, features), BF),
        vm((8, features), F32),
        vm((experts * bucket, tok_dev), BF),
        vm((tok_dev, experts * bucket), BF),
        vm((cap, ne * bucket), BF),
        vm((ne * bucket, cap), BF),
        vm((cap, 128), F32),
        vm((2, tok_dev, feat), BF),
        vm((features, hidden), BF),
        vm((hidden, features), BF),
        vm((2, experts, 2, bucket, share), BF),
        vm((2, ne, bucket, share), BF),
        vm((2, groups, cap, share), BF),
        vm((2, cap, hidden), F32),
        vm((cap, share), F32),
        vm((cap, hidden), BF),
        vm((cap, hidden), BF),
        vm((cap, 128), F32),
        vm((g2, cap, share), BF),
        vm((g2, cap, share), BF),
        vm((RING, half, share), BF),
        vm((2, 2, quarter, share), BF),
        vm((2, 2, half, share), BF),
        vm((2, quarter, share), BF),
        vm((2, half, share), BF),
        vm((half, share), BF),
        vm((8, 128), F32),
        vm((cap, share), BF),
        vm((ne, bucket, share), BF),
        vm((experts, 2, bucket, share), BF),
        vm((nt, 2, 8, share), F32),
        vm((nt, 2, 8, share), F32),
        vm((2, 8, share), F32),
        vm((8, share), F32),
        vm((8, share), F32),
        vm((ne, 8, share), F32),
        vm((experts, feat), F32),
        vm((nt, experts, feat), F32),
        dma(6), dma(2, ne), dma(2, ne), dma(2, 2, 2), dma(2, 2, 2), dma(2, g2, 2, 4), dma(2, groups, 2),
        dma(g2), dma(g2), dma(RING), dma(RING), dma(2, 2), dma(2, 2), dma(2, 2), dma(2, 2),
        dma(2), dma(2), dma(2), dma(2), pltpu.SemaphoreType.DMA, pltpu.SemaphoreType.DMA,
        dma(ne), dma(ne), dma(nt), dma(nt), pltpu.SemaphoreType.DMA, pltpu.SemaphoreType.DMA,
        dma(ne), dma(ne), dma(nt), dma(nt),
    ]
    gt, gin, gout, gr = pl.pallas_call(
        functools.partial(step_kernel, ne, nt, bucket),
        out_shape=(
            jax.ShapeDtypeStruct((tok_dev, feat), BF),
            jax.ShapeDtypeStruct((features, hidden), BF),
            jax.ShapeDtypeStruct((hidden, features), BF),
            jax.ShapeDtypeStruct((experts, features), F32),
        ),
        in_specs=[pl.BlockSpec(memory_space=pltpu.HBM)] * 6,
        out_specs=(vspec,) * 4,
        scratch_shapes=scratch,
        compiler_params=pltpu.CompilerParams(
            collective_id=0, has_side_effects=True, vmem_limit_bytes=48 * 1024 * 1024
        ),
        name="moe_step",
    )(
        tokens, cotangent, w_in, w_out, router.T, chosen,
    )
    gt, gin, gout, gr = hand_out(gt, gin, gout, gr)
    return gt, gin, gout, gr.T


def solution(mesh):
    placed = (
        P("expert", None),
        P("expert", None),
        P(None, ("expert", "tensor")),
        P(("expert", "tensor"), None),
        P(),
        P(),
    )
    return jax.shard_map(
        body,
        mesh=mesh,
        in_specs=placed,
        out_specs=(
            P("expert", "tensor"),
            P(None, ("expert", "tensor")),
            P(("expert", "tensor"), None),
            P(),
        ),
        check_vma=False,
    )
```

```python
import functools

import jax
import jax.numpy as jnp
from jax import lax
from jax.experimental import pallas as pl
from jax.experimental.pallas import tpu as pltpu
from jax.sharding import PartitionSpec as P

MESH = pl.DeviceIdType.MESH
BF = jnp.bfloat16
F32 = jnp.float32
RING = 4


def mm(a, b, dims):
    return lax.dot_general(a, b, (dims, ((), ())), preferred_element_type=F32)


def step_kernel(
    ne, nt, bucket,
    tok, cot, w_in, w_out, rt_any, chosen_any,
    gt, gin, gout, gr,
    chosen, rt, rrow, hot, hot_t, gather, spread, q_col,
    tv, w1v, w2v, sx, rx, gx, acc, gp, hg, da, dsb, rb, cb, zb, yi, yj, yk, yl, zf, fv, fb, es, er,
    rp, rq, rs1, rz, rv, rw, rxs, ry,
    ld, p1s, p1r, pcs, pcr, ags, agr, cs, cr, zzs, zzr, yis, yir, yjs, yjr, yks, ykr, yls, ylr, zfs, zfr,
    rets, retr, r1s, r1r, rzs, rzr, r2s, r2r, r3s, r3r,
):
    me = lax.axis_index("expert")
    t = lax.axis_index("tensor")
    h = me % 2
    y = t // 2
    c = t % 2
    feat = tv.shape[2]
    share = feat // 2
    cap = hg.shape[0]
    groups = gx.shape[1]
    half = cap // 2
    quarter = cap // 4

    zdev = (me + 1 - 2 * h, t)
    cdev = (me, 2 * y + 1 - c)
    yn = (y + 1) % RING
    yp = (y + 3) % RING
    yo = (y + 2) % RING
    ynd = (me, 2 * yn + c)
    ypd = (me, 2 * yp + c)

    def rcopy(src, dst, ss, rs, dev):
        return pltpu.make_async_remote_copy(
            src_ref=src, dst_ref=dst, send_sem=ss, recv_sem=rs, device_id=dev, device_id_type=MESH
        )

    pending = []

    def send(src, dst, ss, rs, dev):
        copy = rcopy(src, dst, ss, rs, dev)
        copy.start()
        pending.append(copy)

    def arrived(dst, rs):
        rcopy(dst, dst, rs, rs, zdev).wait_recv()

    loads = [
        pltpu.make_async_copy(tok.at[:, pl.ds(pl.multiple_of(t * feat, feat), feat)], tv.at[0], ld.at[0]),
        pltpu.make_async_copy(cot.at[:, pl.ds(pl.multiple_of(t * feat, feat), feat)], tv.at[1], ld.at[1]),
        pltpu.make_async_copy(w_in, w1v, ld.at[2]),
        pltpu.make_async_copy(w_out, w2v, ld.at[3]),
    ]
    load_chosen = pltpu.make_async_copy(chosen_any, chosen, ld.at[4])
    load_router = pltpu.make_async_copy(rt_any, rt, ld.at[5])
    load_chosen.start()
    loads[0].start()
    loads[1].start()
    load_router.start()
    loads[2].start()
    loads[3].start()

    barrier = pltpu.get_barrier_semaphore()

    @pl.loop(1, ne)
    def _(d):
        pl.semaphore_signal(barrier, inc=1, device_id=((me + d) % ne, t), device_id_type=MESH)

    @pl.loop(1, nt)
    def _(d):
        pl.semaphore_signal(barrier, inc=1, device_id=(me, (t + d) % nt), device_id_type=MESH)

    experts = chosen.shape[0]
    tok_dev = tv.shape[1]
    slots = experts * bucket
    first = (me * tok_dev).astype(F32)
    col = lax.broadcasted_iota(jnp.int32, (bucket, cap), 1).astype(F32)
    row = lax.broadcasted_iota(jnp.int32, (bucket, cap), 0).astype(F32)
    tok_at = lax.broadcasted_iota(jnp.int32, (bucket, tok_dev), 1).astype(F32)
    load_chosen.wait()
    picks = chosen[...].astype(F32)
    starts = jnp.sum(jnp.where(picks < first, 1.0, 0.0), axis=1, keepdims=True)
    ahead = picks + 1.0
    for k in range(experts):
        match = col == row + starts[k:k + 1, :]
        held = jnp.sum(jnp.where(match, ahead[k:k + 1, :], 0.0), axis=1, keepdims=True) - 1.0 - first
        hot[k * bucket:(k + 1) * bucket, :] = jnp.where(tok_at == held, 1.0, 0.0).astype(BF)

    for a in range(2):
        loads[a].wait()
        for k in range(2):
            packed = mm(hot[...], tv[a, :, k * share:(k + 1) * share], ((1,), (0,))).astype(BF)
            sx[a, :, k] = packed.reshape(slots // bucket, bucket, share)
        if a == 0:
            pl.semaphore_wait(barrier, ne + nt - 2)

        @pl.loop(1, ne)
        def _(d):
            to = (me + d) % ne
            rcopy(sx.at[a, to // 2, to % 2], rx.at[a, me], p1s.at[a, to], p1r.at[a, me], (to, t)).start()

        rx[a, me] = sx[a, me // 2, h]

    home_row = lax.broadcasted_iota(jnp.int32, (ne, cap), 0).astype(F32)
    place = lax.broadcasted_iota(jnp.int32, (ne, cap), 1).astype(F32)
    mine_row = jnp.sum(
        jnp.where(lax.broadcasted_iota(jnp.int32, (experts, cap), 0) == me // 2, chosen[...], 0).astype(F32),
        axis=0, keepdims=True,
    )
    low_bound = home_row * float(tok_dev)
    before = jnp.sum(jnp.where(mine_row < low_bound, 1.0, 0.0), axis=1, keepdims=True)
    inside = jnp.logical_and(mine_row >= low_bound, mine_row < low_bound + float(tok_dev))
    q = jnp.sum(jnp.where(inside, home_row * float(bucket) + place - before, 0.0), axis=0, keepdims=True)
    q_col[...] = jnp.transpose(jnp.broadcast_to(q, (128, cap)))
    load_router.wait()
    router_all = rt[...].astype(F32)
    rrow[...] = jnp.broadcast_to(
        jnp.sum(
            jnp.where(lax.broadcasted_iota(jnp.int32, router_all.shape, 0) == me // 2, router_all, 0.0),
            axis=0, keepdims=True,
        ),
        rrow.shape,
    )

    hot_t[...] = jnp.transpose(hot[...].astype(F32)).astype(BF)
    rows = 128

    @pl.loop(0, cap // rows)
    def _(i):
        at = pl.ds(pl.multiple_of(i * rows, rows), rows)
        slot = lax.broadcasted_iota(jnp.int32, (rows, ne * bucket), 1).astype(F32)
        gather[at, :] = jnp.where(slot == q_col[at, 0:1], 1.0, 0.0).astype(BF)

    @pl.loop(0, ne * bucket // rows)
    def _(i):
        at = pl.ds(pl.multiple_of(i * rows, rows), rows)
        slot = (lax.broadcasted_iota(jnp.int32, (rows, cap), 0) + i * rows).astype(F32)
        spread[at, :] = jnp.where(slot == q, 1.0, 0.0).astype(BF)

    own_g = 4 * y + 2 * c + h

    cut = (half + quarter // 2, half)

    def part_rows(a, part):
        return pl.ds(part * cut[a], cut[a] if part == 0 else cap - cut[a])

    def fan(a, y_, h_, target, part=None):
        g = 4 * y_ + 2 * c + h_
        j = 2 * y_ + h_
        dev = (zdev, ynd, ypd, cdev)[target]
        if part is None:
            ref = gx.at[a, g]
            send(ref, ref, ags.at[a, j, 0, target], agr.at[a, g, 0], dev)
        else:
            ref = gx.at[a, g, part_rows(a, part)]
            send(ref, ref, ags.at[a, j, part, target], agr.at[a, g, part], dev)

    def got(a, y_, h_):
        g = 4 * y_ + 2 * c + h_
        arrived(gx.at[a, g], agr.at[a, g, 0])

    def got_halves(a, y_, h_):
        g = 4 * y_ + 2 * c + h_
        for part in range(2):
            arrived(gx.at[a, g, part_rows(a, part)], agr.at[a, g, part])

    Z, N, B, C = 0, 1, 2, 3

    buckets = ne * bucket
    def dispatched(a):
        @pl.loop(1, ne)
        def _(d):
            source = (me + ne - d) % ne
            arrived(rx.at[a, source], p1r.at[a, source])

    def compact(a):
        @pl.loop(0, cap // rows)
        def _(i):
            at = pl.ds(pl.multiple_of(i * rows, rows), rows)
            gx[a, own_g, at] = mm(gather[at, :], rx[a].reshape(buckets, share), ((1,), (0,))).astype(BF)

    acc[...] = jnp.zeros_like(acc)
    gp[...] = jnp.zeros_like(gp)

    def block_at(g):
        return pl.ds(pl.multiple_of(g * share, share), share)

    def add_x(g):
        x = gx[0, g]
        acc[0] += mm(x, w1v[block_at(g), :], ((1,), (0,)))
        gp[...] += x.astype(F32) * rrow[0:1, block_at(g)]

    def add_y(g):
        acc[1] += mm(gx[1, g], w2v[:, block_at(g)], ((1,), (1,)))

    def use(a, y_):
        @pl.loop(0, 2)
        def _(k):
            g = 4 * y_ + 2 * c + k
            o = 4 * y_ + 2 * (1 - c) + k
            (add_x, add_y)[a](g)
            arrived(gx.at[a, o], agr.at[a, o, 0])
            (add_x, add_y)[a](o)

    def got_half(a, y_, h_, part):
        g = 4 * y_ + 2 * c + h_
        arrived(gx.at[a, g, part_rows(a, part)], agr.at[a, g, part])

    def piece(a, y_, h_, part, k):
        g = 4 * y_ + 2 * c + h_
        whole = part_rows(a, part)
        return gx.at[a, g, pl.ds(whole.start + k * (whole.size // 2), whole.size // 2)]

    def relay(y_, h_, part, k, target):
        ref = piece(0, y_, h_, part, k)
        send(ref, ref, pcs.at[h_, part, k], pcr.at[h_, part, k], (zdev, ynd, ypd, cdev)[target])

    def got_pieces(y_, h_, part):
        for k in range(2):
            arrived(piece(0, y_, h_, part, k), pcr.at[h_, part, k])

    dispatched(0)
    compact(0)
    fan(0, y, h, N, 1)
    fan(0, y, h, B, 1)
    fan(0, y, h, N, 0)
    fan(0, y, h, B, 0)
    fan(0, y, h, Z, 1)
    fan(0, y, h, Z, 0)
    fan(0, y, h, C)
    for part in (1, 0):
        got_half(0, yp, h, part)
        relay(yp, h, part, 0, N)
        got_half(0, yn, h, part)
        relay(yn, h, part, 1, B)
    fan(0, yp, h, C)
    fan(0, yn, h, C)
    dispatched(1)
    compact(1)
    fan(1, y, h, Z)
    fan(1, y, h, N)
    fan(1, y, h, B)
    fan(1, y, h, C)
    fan(0, yp, h, Z, 0)
    fan(0, yn, h, Z, 0)
    got_pieces(yo, h, 0)
    fan(0, yo, h, Z, 0)
    got_pieces(yo, h, 1)
    fan(0, yo, h, C)
    loads[2].wait()
    got_half(0, y, 1 - h, 1)
    fan(0, y, 1 - h, N, 1)
    fan(0, y, 1 - h, B, 1)
    got(1, yp, h)
    fan(1, yp, h, N, 0)
    fan(1, yp, h, C)
    got(1, yn, h)
    fan(1, yn, h, B, 1)
    fan(1, yn, h, C)
    got(1, y, 1 - h)
    fan(1, y, 1 - h, N)
    fan(1, y, 1 - h, B)
    fan(1, y, 1 - h, C)
    got_half(0, y, 1 - h, 0)
    fan(0, y, 1 - h, C)
    use(0, y)
    loads[3].wait()
    got_half(0, yp, 1 - h, 1)
    relay(yp, 1 - h, 1, 0, N)
    got_half(0, yn, 1 - h, 1)
    relay(yn, 1 - h, 1, 1, B)
    use(1, y)
    got_halves(1, yo, h)
    fan(1, yo, h, C)
    got_half(0, yp, 1 - h, 0)
    fan(0, yp, 1 - h, C)
    got_half(0, yn, 1 - h, 0)
    fan(0, yn, 1 - h, C)
    use(0, yp)
    got(1, yp, 1 - h)
    fan(1, yp, 1 - h, N, 0)
    fan(1, yp, 1 - h, C)
    got(1, yn, 1 - h)
    fan(1, yn, 1 - h, B, 1)
    fan(1, yn, 1 - h, C)
    use(0, yn)
    got_half(0, yo, 1 - h, 0)
    got_pieces(yo, 1 - h, 1)
    fan(0, yo, 1 - h, C)
    use(1, yp)
    use(0, yo)
    use(1, yn)
    got_halves(1, yo, 1 - h)
    fan(1, yo, 1 - h, C)
    use(1, yo)

    er_rows = 64

    @pl.loop(0, cap // er_rows)
    def _(i):
        at = pl.ds(pl.multiple_of(i * er_rows, er_rows), er_rows)
        gate = jax.nn.sigmoid(jnp.sum(gp[at, :], axis=1, keepdims=True))
        pre = acc[0, at, :]
        up = acc[1, at, :]
        sig = jax.nn.sigmoid(pre)
        hidden = pre * sig
        hg[at, :] = (gate * hidden).astype(BF)
        gate_grad = jnp.sum(hidden * up, axis=1, keepdims=True)
        da[at, :] = (gate * up * sig * (1.0 + pre * (1.0 - sig))).astype(BF)
        score = gate_grad * gate * (1.0 - gate)
        dsb[at, :] = jnp.broadcast_to(score, (er_rows, dsb.shape[1]))

    def r_value(g):
        s = dsb[...]
        wide = jnp.concatenate([s, s], axis=1)
        return mm(da[...], w1v[block_at(g), :], ((1,), (1,))) + wide * rrow[0:1, block_at(g)]

    low = pl.ds(0, half)
    high = pl.ds(half, half)

    def partner(place_y):
        @pl.loop(0, 2)
        def _(k):
            i = 2 * place_y + k
            rb[i] = r_value(4 * place_y + 2 * (1 - c) + k).astype(BF)
            rcopy(rb.at[i], cb.at[i], cs.at[i], cr.at[i], cdev).start()

    def sums(place_y):
        @pl.loop(0, 2)
        def _(k):
            j = 2 * place_y + k
            value = r_value(4 * place_y + 2 * c + k)
            arrived(cb.at[j], cr.at[j])
            cb[j] = (cb[j].astype(F32) + value).astype(BF)

        send(cb.at[2 * place_y + 1 - h, low], zb.at[place_y], zzs.at[place_y], zzr.at[place_y], zdev)

    partner(yo)
    partner(yp)
    sums(yo)
    for k in range(2):
        send(cb.at[2 * yo + k, pl.ds(half, quarter)], yi.at[k, 0], yis.at[k, 0], yir.at[k, 0], ynd)
        send(cb.at[2 * yo + k, pl.ds(half + quarter, quarter)], yi.at[k, 1], yis.at[k, 1], yir.at[k, 1], ypd)
    partner(yn)
    sums(yp)
    partner(y)
    sums(yn)
    sums(y)

    def add_z(k):
        arrived(zb.at[k], zzr.at[k])
        zb[k] = (zb[k].astype(F32) + cb[2 * k + h, low].astype(F32)).astype(BF)

    add_z(yo)
    send(zb.at[yo, pl.ds(0, quarter)], yk.at[0], yks.at[0], ykr.at[0], ynd)
    send(zb.at[yo, pl.ds(quarter, quarter)], yk.at[1], yks.at[1], ykr.at[1], ypd)
    for k in range(2):
        arrived(yi.at[k, 0], yir.at[k, 0])
        arrived(yi.at[k, 1], yir.at[k, 1])
        first = pl.ds(half, quarter)
        second = pl.ds(half + quarter, quarter)
        cb[2 * yn + k, first] = (cb[2 * yn + k, first].astype(F32) + yi[k, 0].astype(F32)).astype(BF)
        cb[2 * yp + k, second] = (cb[2 * yp + k, second].astype(F32) + yi[k, 1].astype(F32)).astype(BF)
        send(cb.at[2 * yn + k, high], yj.at[k, 0], yjs.at[k, 0], yjr.at[k, 0], ynd)
        send(cb.at[2 * yp + k, high], yj.at[k, 1], yjs.at[k, 1], yjr.at[k, 1], ypd)

    s = dsb[...]
    s_hi = s.astype(BF).astype(F32)
    s_mid = (s - s_hi).astype(BF).astype(F32)
    s_lo = s - s_hi - s_mid
    lane = lax.broadcasted_iota(jnp.int32, s.shape, 1)
    terms = jnp.where(lane == 0, s_hi, jnp.where(lane == 1, s_mid, jnp.where(lane == 2, s_lo, 0.0)))
    terms = jnp.transpose(terms)[:16].astype(BF)

    @pl.loop(0, groups)
    def _(g):
        rp[g // 2, g % 2] = mm(terms, gx[0, g], ((1,), (0,)))[:8]

    @pl.loop(1, nt)
    def _(d):
        to = (t + d) % nt
        rcopy(rp.at[to], rq.at[t], r1s.at[to], r1r.at[t], (me, to)).start()

    def weight_grads(first, count):
        @pl.loop(first, first + count)
        def _(g):
            gout[:, block_at(g)] = mm(hg[...], gx[1, g], ((0,), (0,))).astype(BF)
            gin[block_at(g), :] = mm(gx[0, g], da[...], ((0,), (0,))).astype(BF)

    @pl.loop(1, nt)
    def _(d):
        source = (t + nt - d) % nt
        arrived(rq.at[source], r1r.at[source])

    rq[t] = rp[t]
    total = rq[0]
    for k in range(1, nt):
        total = total + rq[k]
    rs1[...] = total
    send(rs1.at[1 - h], rz, rzs, rzr, zdev)

    weight_grads(0, 4)
    add_z(yp)
    add_z(yn)
    first = pl.ds(0, quarter)
    second = pl.ds(quarter, quarter)
    for k in range(2):
        arrived(yk.at[k], ykr.at[k])
    zb[yn, first] = (zb[yn, first].astype(F32) + yk[0].astype(F32)).astype(BF)
    zb[yp, second] = (zb[yp, second].astype(F32) + yk[1].astype(F32)).astype(BF)
    send(zb.at[yn], yl.at[0], yls.at[0], ylr.at[0], ynd)
    send(zb.at[yp], yl.at[1], yls.at[1], ylr.at[1], ypd)
    base = 2 * y + 1 - h
    for k in range(2):
        for n in range(2):
            arrived(yj.at[k, n], yjr.at[k, n])
    cb[base, high] = (
        cb[base, high].astype(F32) + (yj[1 - h, 0].astype(F32) + yj[1 - h, 1].astype(F32))
    ).astype(BF)
    send(cb.at[base, high], zf, zfs, zfr, zdev)

    weight_grads(4, 6)

    mine = 2 * y + h
    arrived(zb.at[y], zzr.at[y])
    arrived(zf, zfr)
    fb[high, :] = (
        cb[mine, high].astype(F32) + (yj[h, 0].astype(F32) + yj[h, 1].astype(F32)) + zf[...].astype(F32)
    ).astype(BF)
    for side in range(2):
        arrived(yl.at[side], ylr.at[side])
    fb[low, :] = (
        cb[mine, low].astype(F32) + zb[y].astype(F32) + (yl[0].astype(F32) + yl[1].astype(F32))
    ).astype(BF)

    arrived(rz, rzr)
    router_sum = jnp.sum(rs1[h] + rz[...], axis=0, keepdims=True)
    rv[...] = jnp.broadcast_to(router_sum, rv.shape)
    rw[me] = jnp.broadcast_to(router_sum, rv.shape)

    @pl.loop(1, ne)
    def _(d):
        to = (me + d) % ne
        rcopy(rv, rw.at[me], r2s.at[to], r2r.at[me], (to, t)).start()

    homes = rows // bucket

    @pl.loop(0, ne // homes)
    def _(i):
        chunk = (i + me // homes) % (ne // homes)
        at = pl.ds(pl.multiple_of(chunk * rows, rows), rows)
        es[pl.ds(chunk * homes, homes)] = (
            mm(spread[at, :], fb[...], ((1,), (0,))).astype(BF).reshape(homes, bucket, share)
        )

        @pl.loop(0, homes)
        def _(k):
            to = chunk * homes + (me + k) % homes

            @pl.when(to != me)
            def _():
                rcopy(es.at[to], er.at[me // 2, h], rets.at[to], retr.at[me], (to, t)).start()

    er[me // 2, h] = es[me]

    weight_grads(10, 6)
    @pl.loop(1, ne)
    def _(d):
        source = (me + ne - d) % ne
        arrived(rw.at[source], r2r.at[source])

    for k in range(ne):
        rxs[k // 2:k // 2 + 1, (k % 2) * share:(k % 2 + 1) * share] = rw[k, 0:1, :]
    ry[t] = rxs[...]

    @pl.loop(1, nt)
    def _(d):
        to = (t + d) % nt
        rcopy(rxs, ry.at[t], r3s.at[to], r3r.at[t], (me, to)).start()

    @pl.loop(1, nt)
    def _(d):
        source = (t + nt - d) % nt
        arrived(ry.at[source], r3r.at[source])

    for k in range(nt):
        gr[:, k * feat:(k + 1) * feat] = ry[k]

    @pl.loop(1, ne)
    def _(d):
        source = (me + ne - d) % ne
        arrived(er.at[source // 2, source % 2], retr.at[source])

    for k in range(2):
        gt[:, k * share:(k + 1) * share] = mm(hot_t[...], er[:, k].reshape(slots, share), ((1,), (0,))).astype(BF)

    @pl.loop(1, ne)
    def _(d):
        to = (me + d) % ne
        for a in range(2):
            rcopy(sx.at[a, 0, 0], rx.at[a, 0], p1s.at[a, to], p1r.at[a, to], zdev).wait_send()
        rcopy(rv, rw.at[0], r2s.at[to], r2r.at[to], zdev).wait_send()
        rcopy(es.at[0], er.at[0, 0], rets.at[to], retr.at[to], zdev).wait_send()

    @pl.loop(1, nt)
    def _(d):
        to = (t + d) % nt
        rcopy(rp.at[0], rq.at[0], r1s.at[to], r1r.at[to], zdev).wait_send()
        rcopy(rxs, ry.at[0], r3s.at[to], r3r.at[to], zdev).wait_send()

    @pl.loop(0, groups // 2)
    def _(j):
        rcopy(rb.at[j], cb.at[j], cs.at[j], cr.at[j], zdev).wait_send()

    for copy in pending:
        copy.wait_send()


def hand_kernel(*refs):
    ins, outs = refs[:4], refs[4:8]
    copies = [pltpu.make_async_copy(a, b, refs[8].at[n]) for n, (a, b) in enumerate(zip(ins, outs))]
    for copy in copies:
        copy.start()
    for copy in copies:
        copy.wait()


def hand_out(*arrays):
    aspec = pl.BlockSpec(memory_space=pl.ANY)
    vspec = pl.BlockSpec(memory_space=pltpu.VMEM)
    return pl.pallas_call(
        hand_kernel,
        out_shape=tuple(jax.ShapeDtypeStruct(v.shape, v.dtype) for v in arrays),
        in_specs=[vspec] * 4,
        out_specs=(aspec,) * 4,
        scratch_shapes=[pltpu.SemaphoreType.DMA((4,))],
        compiler_params=pltpu.CompilerParams(vmem_limit_bytes=16 * 1024 * 1024),
        name="hand_out",
    )(*arrays)


def body(tokens, cotangent, w_in, w_out, router, chosen):
    tok_dev, features = tokens.shape
    hidden = w_in.shape[1]
    ne = lax.axis_size("expert")
    nt = lax.axis_size("tensor")
    bucket = 4 * tok_dev // ne
    experts, cap = chosen.shape
    feat = features // nt
    share = feat // 2
    groups = features // share

    vm = lambda shape, kind: pltpu.VMEM(shape, kind)
    dma = lambda *shape: pltpu.SemaphoreType.DMA(shape)
    vspec = pl.BlockSpec(memory_space=pltpu.VMEM)
    aspec = pl.BlockSpec(memory_space=pl.ANY)
    half, quarter = cap // 2, cap // 4
    g2 = groups // 2
    scratch = [
        vm((experts, cap), jnp.int32),
        vm((experts, features), BF),
        vm((8, features), F32),
        vm((experts * bucket, tok_dev), BF),
        vm((tok_dev, experts * bucket), BF),
        vm((cap, ne * bucket), BF),
        vm((ne * bucket, cap), BF),
        vm((cap, 128), F32),
        vm((2, tok_dev, feat), BF),
        vm((features, hidden), BF),
        vm((hidden, features), BF),
        vm((2, experts, 2, bucket, share), BF),
        vm((2, ne, bucket, share), BF),
        vm((2, groups, cap, share), BF),
        vm((2, cap, hidden), F32),
        vm((cap, share), F32),
        vm((cap, hidden), BF),
        vm((cap, hidden), BF),
        vm((cap, 128), F32),
        vm((g2, cap, share), BF),
        vm((g2, cap, share), BF),
        vm((RING, half, share), BF),
        vm((2, 2, quarter, share), BF),
        vm((2, 2, half, share), BF),
        vm((2, quarter, share), BF),
        vm((2, half, share), BF),
        vm((half, share), BF),
        vm((8, 128), F32),
        vm((cap, share), BF),
        vm((ne, bucket, share), BF),
        vm((experts, 2, bucket, share), BF),
        vm((nt, 2, 8, share), F32),
        vm((nt, 2, 8, share), F32),
        vm((2, 8, share), F32),
        vm((8, share), F32),
        vm((8, share), F32),
        vm((ne, 8, share), F32),
        vm((experts, feat), F32),
        vm((nt, experts, feat), F32),
        dma(6), dma(2, ne), dma(2, ne), dma(2, 2, 2), dma(2, 2, 2), dma(2, g2, 2, 4), dma(2, groups, 2),
        dma(g2), dma(g2), dma(RING), dma(RING), dma(2, 2), dma(2, 2), dma(2, 2), dma(2, 2),
        dma(2), dma(2), dma(2), dma(2), pltpu.SemaphoreType.DMA, pltpu.SemaphoreType.DMA,
        dma(ne), dma(ne), dma(nt), dma(nt), pltpu.SemaphoreType.DMA, pltpu.SemaphoreType.DMA,
        dma(ne), dma(ne), dma(nt), dma(nt),
    ]
    gt, gin, gout, gr = pl.pallas_call(
        functools.partial(step_kernel, ne, nt, bucket),
        out_shape=(
            jax.ShapeDtypeStruct((tok_dev, feat), BF),
            jax.ShapeDtypeStruct((features, hidden), BF),
            jax.ShapeDtypeStruct((hidden, features), BF),
            jax.ShapeDtypeStruct((experts, features), F32),
        ),
        in_specs=[pl.BlockSpec(memory_space=pltpu.HBM)] * 6,
        out_specs=(vspec,) * 4,
        scratch_shapes=scratch,
        compiler_params=pltpu.CompilerParams(
            collective_id=0, has_side_effects=True, vmem_limit_bytes=48 * 1024 * 1024
        ),
        name="moe_step",
    )(
        tokens, cotangent, w_in, w_out,
        pltpu.with_memory_space_constraint(router.T, pltpu.HBM),
        pltpu.with_memory_space_constraint(chosen, pltpu.HBM),
    )
    gt, gin, gout, gr = hand_out(gt, gin, gout, gr)
    return gt, gin, gout, gr.T


def solution(mesh):
    placed = (
        P("expert", None),
        P("expert", None),
        P(None, ("expert", "tensor")),
        P(("expert", "tensor"), None),
        P(),
        P(),
    )
    return jax.shard_map(
        body,
        mesh=mesh,
        in_specs=placed,
        out_specs=(
            P("expert", "tensor"),
            P(None, ("expert", "tensor")),
            P(("expert", "tensor"), None),
            P(),
        ),
        check_vma=False,
    )
```
